32 devices in a mesh: row: 8 (over y, x, core), col: 4 (over z).
Axes of the slice: x: 2, y: 2, z: 4, core: 2. Of those that a mesh axis runs over, the one named last changes fastest.
Arguments:
- hidden: bfloat16 [4128, 1792], P('row', 'col'), may hold values from -6 to 6
- norm_gain: bfloat16 [1792], P('col'), may hold values from 0.099609375 to 1.8984375
- qkv_weight: bfloat16 [1792, 2304], P('row', 'col'), may hold values from -0.125 to 0.125
- out_weight: bfloat16 [1792, 1792], P('col', 'row'), may hold values from -1.5 to 1.5
- cache: bfloat16 [40, 1024, 2048], P('row', None, 'col'), may hold values from -6 to 6
- cached: int32 [40], P('row'), may hold values from 128 to 1024, as said below
- token_mask: int32 [4128], P('row'), may hold values 0 or 1
Outputs:
- mixed: bfloat16 [4128, 1792], P('row', 'col')
The draws below stay inside these ranges and needn't reach their ends.
Inputs may be any that keep to these rules, and one draw needn't show every extreme that they name: Some request has exactly 1024 cached positions.
All inputs are finite; a program needn't handle non-finite values. No bound on the sum of `token_mask` on one device may be relied on, other than what follows from the above.
Results may differ from the reference program's by a relative error of at most 0.0072.
Values may be sent and summed in bfloat16 or wider, within the bound.
No kernel may reach another device: no remote copies, remote signals or barrier semaphores. Data moves between devices by JAX's collectives and lax.ppermute only.
A program may use at most 64 MiB of HBM per device.

```python
import jax
import jax.numpy as jnp
from jax import lax

D = 1792
HEADS = 16
FEATURE_WIDTH = 16
HDIM = 112
SPAN_TOKENS = 512
DEC = 4
CAP = 1024
MINLEN = 128
QKV = 2304
HD = 1792
REQS = 40
TOKENS = 4128
N_ROW = 8


def draw_cached(key, part):
    key_long, key_short, key_pick, key_top = jax.random.split(key, 4)
    longer = jax.random.randint(key_long, (REQS,), MINLEN, CAP + 1)
    shorter = jax.random.randint(key_short, (REQS,), MINLEN, 2 * MINLEN + 1)
    picked = jax.random.randint(key_pick, (REQS,), 0, 4)
    values = jnp.where(picked == 0, longer, shorter)
    topmost = jax.random.randint(key_top, (), 0, REQS)
    values = jnp.where(jnp.arange(REQS) == topmost, CAP, values)
    return values.astype(jnp.int32)


def touch_ends(drawn, rng, least, largest):
    shape = drawn.shape
    place = [jax.random.randint(jax.random.fold_in(rng, axis), (), 0, shape[axis]) for axis in range(len(shape))]
    drawn = drawn.at[tuple(place)].set(least)
    longest = shape.index(max(shape))
    place[longest] = (place[longest] + 1) % shape[longest]
    return drawn.at[tuple(place)].set(largest)


def steps_of(own_key, extent, cuts, smallest, largest):
    factor_of = 1.0
    for dim, blocks in cuts:
        draws = jax.random.uniform(jax.random.fold_in(jax.random.fold_in(own_key, 6), dim), (blocks,), jnp.float32, smallest / len(cuts), largest / len(cuts))
        factor_of = factor_of * jnp.repeat(jnp.exp(draws), extent[dim] // blocks).reshape((-1,) + (1,) * (len(extent) - 1 - dim))
    return factor_of


def scatter_about(key, extent, scale, most, cuts=(), kind=jnp.bfloat16):
    gain = steps_of(key, extent, cuts, -0.22, 0.18) if cuts else 1.0
    entries = jax.random.normal(key, extent, jnp.float32) * scale * gain
    return jnp.minimum(jnp.maximum(entries, -most), most).astype(kind)


def setup_inputs(seed: int = 0) -> dict:
    seeds = jax.random.split(jax.random.key(seed), 8)
    return {
        "hidden": scatter_about(seeds[0], (TOKENS, D), 1.0, 6.0, ((0, 8), (1, 4))),
        "norm_gain": jnp.clip(1.0 + 0.18 * jax.random.normal(seeds[1], (D,), jnp.float32), 0.099609375, 1.8984375).astype(jnp.bfloat16),
        "qkv_weight": scatter_about(seeds[2], (D, QKV), D ** -0.5, 0.125, ((0, 8), (1, 4))),
        "out_weight": scatter_about(seeds[3], (HD, D), (HDIM // 8) ** -0.5, 1.5, ((0, 4), (1, 8))),
        "cache": scatter_about(seeds[4], (REQS, CAP, HEADS * (FEATURE_WIDTH + HDIM)), 1.0, 6.0, ((0, 8), (2, 4))),
        "cached": draw_cached(jax.random.fold_in(seeds[7], 71), 0),
        "token_mask": touch_ends((jax.random.randint(seeds[6], (TOKENS,), 0, 8) < 7).astype(jnp.int32), jax.random.fold_in(seeds[6], 1), 0, 1),
    }


def taylor(taylor_score):
    return 1.0 + taylor_score + 0.5 * taylor_score * taylor_score

def one_group(item):
    proj, mask, store, lens = item
    live = mask.astype(jnp.float32)
    score_scale = FEATURE_WIDTH ** (-0.5)
    query_rows = proj[:, :, :FEATURE_WIDTH].astype(jnp.float32)
    key_rows = proj[:, :, FEATURE_WIDTH:2 * FEATURE_WIDTH].astype(jnp.float32)
    values = proj[:, :, 2 * FEATURE_WIDTH:].astype(jnp.float32)
    position = jnp.arange(CAP, dtype=jnp.int32)
    prior_tokens = store[0].astype(jnp.float32)
    taylor_score = jnp.einsum('sue,pue->usp', query_rows[:SPAN_TOKENS], prior_tokens[:, :, :FEATURE_WIDTH]) * score_scale
    weight = taylor(taylor_score) * (position < lens[0]).astype(jnp.float32)[None, None, :]
    numer = jnp.einsum('hqk,khd->hqd', weight.astype(jnp.bfloat16).astype(jnp.float32), prior_tokens[:, :, FEATURE_WIDTH:])
    denom = lax.optimization_barrier(jnp.sum(weight, axis=-1))
    taylor_score = jnp.einsum('sue,pue->usp', query_rows[:SPAN_TOKENS], key_rows[:SPAN_TOKENS]) * score_scale
    order = jnp.arange(SPAN_TOKENS, dtype=jnp.int32)
    allowed = (order[None, :] <= order[:, None]).astype(jnp.float32) * live[:SPAN_TOKENS][None, :]
    weight = taylor(taylor_score) * allowed[None]
    numer = numer + jnp.einsum('hqk,khd->hqd', weight.astype(jnp.bfloat16).astype(jnp.float32), values[:SPAN_TOKENS])
    denom = denom + lax.optimization_barrier(jnp.sum(weight, axis=-1))
    past = store[1:].astype(jnp.float32)
    taylor_score = jnp.einsum('rhf,rkhf->rhk', query_rows[SPAN_TOKENS:], past[..., :FEATURE_WIDTH]) * score_scale
    seen = (position[None, :] < lens[1:, None]).astype(jnp.float32)
    weight = taylor(taylor_score) * seen[:, None, :]
    dec_numer = jnp.einsum('rhk,rkhd->rhd', weight.astype(jnp.bfloat16).astype(jnp.float32), past[..., FEATURE_WIDTH:])
    dec_denom = lax.optimization_barrier(jnp.sum(weight, axis=-1))
    taylor_score = lax.optimization_barrier(jnp.sum(query_rows[SPAN_TOKENS:] * key_rows[SPAN_TOKENS:], axis=-1)) * score_scale
    weight = taylor(taylor_score) * live[SPAN_TOKENS:, None]
    dec_numer = dec_numer + weight.astype(jnp.bfloat16).astype(jnp.float32)[..., None] * values[SPAN_TOKENS:]
    dec_denom = dec_denom + weight
    numer_all = jnp.concatenate([jnp.transpose(numer, (1, 0, 2)), dec_numer], axis=0)
    denom_all = jnp.concatenate([jnp.transpose(denom, (1, 0)), dec_denom], axis=0)
    result = live[:, None, None] * numer_all / (denom_all + 1.0 - live[:, None])[..., None]
    return result.astype(jnp.bfloat16)

def reference(hidden, norm_gain, qkv_weight, out_weight, cache, cached, token_mask):
    wide = hidden.astype(jnp.float32)
    normed = wide * lax.rsqrt(lax.optimization_barrier(jnp.mean(wide * wide, axis=-1, keepdims=True)) + 1e-06) * norm_gain.astype(jnp.float32)
    normed = normed.astype(jnp.bfloat16)
    projected = jnp.dot(normed, qkv_weight, preferred_element_type=jnp.float32).astype(jnp.bfloat16)
    per_row = SPAN_TOKENS + DEC
    groups = projected.reshape(N_ROW, per_row, HEADS, 2 * FEATURE_WIDTH + HDIM)
    masks = token_mask.reshape(N_ROW, per_row)
    stores = cache.reshape(N_ROW, 1 + DEC, CAP, HEADS, FEATURE_WIDTH + HDIM)
    lens = cached.reshape(N_ROW, 1 + DEC)
    attended = lax.map(one_group, (groups, masks, stores, lens))
    attended = attended.reshape(TOKENS, HEADS * HDIM)
    return jnp.dot(attended, out_weight, preferred_element_type=jnp.float32).astype(jnp.bfloat16)
```

```python
import jax
import jax.numpy as jnp
from jax import lax
from jax.experimental import pallas as pl
from jax.experimental.pallas import tpu as pltpu
from jax.sharding import PartitionSpec as P

FEATURE_WIDTH = 16
HDIM = 112
SPAN_TOKENS = 512
DEC = 4
LANES = FEATURE_WIDTH + HDIM
F32 = jnp.float32
BF16 = jnp.bfloat16
HALF = SPAN_TOKENS // 2
VMEM = pl.BlockSpec(memory_space=pltpu.VMEM)
SMEM = pl.BlockSpec(memory_space=pltpu.SMEM)
ANY = pl.BlockSpec(memory_space=pl.ANY)
TAIL = 3 * HALF
BODY = TAIL + HALF // 2
EXTRA = 32
QROWS = 224
OROWS = 448


def gray(place):
    return place ^ (place >> 1)


def call(body, outs, in_specs, scratch=(), flops=0, nbytes=0, name=None):
    return pl.pallas_call(
        body,
        out_shape=outs,
        in_specs=in_specs,
        out_specs=jax.tree.map(lambda _: VMEM, outs),
        scratch_shapes=scratch,
        cost_estimate=pl.CostEstimate(flops=flops, bytes_accessed=nbytes, transcendentals=0),
        compiler_params=pltpu.CompilerParams(vmem_limit_bytes=48 * 1024 * 1024),
        name=name,
    )


def shaped(shape, dtype=BF16):
    return jax.ShapeDtypeStruct(shape, dtype)


def dot(a, b):
    return jnp.dot(a, b, preferred_element_type=F32)


def dot_nt(a, b):
    return lax.dot_general(a, b, (((1,), (1,)), ((), ())), preferred_element_type=F32)


def lane(shape):
    return lax.broadcasted_iota(jnp.int32, shape, len(shape) - 1)


def row(shape):
    return lax.broadcasted_iota(jnp.int32, shape, 0)


def pack_tokens(h_ref, g_ref, a_ref, b_ref):
    for ref, base in ((a_ref, 0), (b_ref, HALF)):
        for t in range(3):
            ref[t * HALF : (t + 1) * HALF, :] = h_ref[base : base + HALF, t * 128 : (t + 1) * 128]
        low = h_ref[base : base + HALF // 2, 384:448]
        high = h_ref[base + HALF // 2 : base + HALF, 384:448]
        ref[TAIL:BODY, :] = jnp.concatenate([low, high], axis=1)
        ref[BODY:, :] = jnp.zeros((EXTRA, 128), BF16)
    for t in range(3):
        a_ref[BODY + 8 * t : BODY + 8 * t + 1, :] = g_ref[:, t * 128 : (t + 1) * 128]
        b_ref[BODY + 8 * t : BODY + 8 * t + DEC, :] = h_ref[SPAN_TOKENS:, t * 128 : (t + 1) * 128]
    last = g_ref[:, 384:448]
    a_ref[BODY + 24 : BODY + 25, :] = jnp.concatenate([last, last], axis=1)
    b_ref[BODY + 24 : BODY + 24 + DEC, 0:64] = h_ref[SPAN_TOKENS:, 384:448]


def pack_weights(q_ref, o_ref, w_ref):
    width = FEATURE_WIDTH + LANES
    for h in range(4):
        w_ref[h * QROWS : (h + 1) * QROWS, :] = q_ref[:, h * width + FEATURE_WIDTH : (h + 1) * width]
    queries = [q_ref[:, h * width : h * width + FEATURE_WIDTH] for h in range(4)]
    w_ref[4 * QROWS : 5 * QROWS, :] = jnp.concatenate(
        queries + [jnp.zeros((QROWS, 64), BF16)], axis=1
    )
    w_ref[5 * QROWS : 5 * QROWS + OROWS, :] = o_ref[:, 0:128]
    w_ref[5 * QROWS + OROWS :, :] = jnp.concatenate(
        [o_ref[:, 128:224], jnp.zeros((OROWS, 32), BF16)], axis=1
    )


def place_weights(*refs):
    blocks, (q_ref, o_ref) = refs[:8], refs[8:]
    me = lax.axis_index("row")
    for k in range(8):
        owner = me ^ k
        part, side = owner >> 1, owner & 1
        start = pl.multiple_of(side * QROWS, 32)
        for t in range(5):
            q_ref[part, pl.ds(start, QROWS), t * 128 : (t + 1) * 128] = blocks[k][
                t * QROWS : (t + 1) * QROWS, :
            ]

        @pl.when(side == 1)
        def _():
            for t in range(5):
                q_ref[part, 448:512, t * 128 : (t + 1) * 128] = blocks[k][
                    t * QROWS + 160 : (t + 1) * QROWS, :
                ]

    def outs(k, low, high):
        part = (me ^ k) >> 1
        at = 5 * QROWS
        full = jnp.concatenate(
            [
                low[at : at + OROWS, :],
                low[at + OROWS :, 0:96],
                high[at : at + OROWS, :],
                high[at + OROWS :, 0:96],
            ],
            axis=1,
        )
        full = jnp.concatenate([full, full[:, 384:448]], axis=1)
        for h in range(4):
            o_ref[part, h * LANES : h * LANES + FEATURE_WIDTH, :] = jnp.zeros(
                (FEATURE_WIDTH, 512), BF16
            )
            o_ref[part, h * LANES + FEATURE_WIDTH : (h + 1) * LANES, :] = full[
                h * HDIM : (h + 1) * HDIM, :
            ]

    for k in (0, 2, 4, 6):

        @pl.when((me & 1) == 0)
        def _():
            outs(k, blocks[k], blocks[k + 1])

        @pl.when((me & 1) == 1)
        def _():
            outs(k, blocks[k + 1], blocks[k])


def as_keys(kv):
    return jnp.where(lane(kv.shape) % LANES == FEATURE_WIDTH, 1.0, kv).astype(BF16)


def as_values(kv, keep):
    ones = jnp.where(lane(kv.shape) % LANES < FEATURE_WIDTH, 1.0, kv)
    return jnp.where(keep, ones, 0.0).astype(BF16)


def prepare_cache(cache, len_ref, k_ref, v_ref, slab, sem):
    copy = pltpu.make_async_copy(cache.at[0], slab, sem)
    copy.start()
    copy.wait()
    kv = slab[...].astype(F32)
    k_ref[...] = as_keys(kv)
    v_ref[...] = as_values(kv, row(kv.shape) < len_ref[0])


def project(blocks, gain_ref, w_ref, rows):
    place = gray(lax.axis_index("col"))
    middle = lane((HALF // 2, 128)) < 64
    pieces, square = [], None
    for ref in blocks:
        tail = ref[TAIL:BODY, :].astype(F32)
        tail = jnp.concatenate([jnp.where(middle, tail, 0.0), jnp.where(middle, 0.0, tail)], axis=0)
        tiles = [ref[t * HALF : (t + 1) * HALF, :].astype(F32) for t in range(3)] + [tail]
        if rows > HALF:
            tiles = [
                jnp.concatenate(
                    [
                        tile,
                        ref[BODY + 8 * t : BODY + 8 * t + 8, :].astype(F32),
                        jnp.zeros((8, 128), F32),
                    ],
                    axis=0,
                )
                for t, tile in enumerate(tiles)
            ]
        pieces.append(tiles)
        for tile in tiles:
            square = tile * tile if square is None else square + tile * tile
    mean = jnp.sum(square, axis=1, keepdims=True) * (1.0 / 1792.0)
    scale = jnp.broadcast_to(lax.rsqrt(mean + 1e-06), (rows, 128))
    total = None
    for k, tiles in enumerate(pieces):
        source = gray((place + 4 - k) & 3)
        normed = [
            (tile * scale * gain_ref[k][BODY + 8 * t : BODY + 8 * t + 1, :].astype(F32)).astype(BF16)
            for t, tile in enumerate(tiles)
        ]
        term = dot(jnp.concatenate(normed, axis=1), w_ref[source])
        total = term if total is None else total + term
    total = total.astype(BF16).astype(F32)
    return total[:, 0:512], total[:, 512:640]


def query_of(queries, h):
    q = pltpu.roll(queries, (128 - FEATURE_WIDTH * h) % 128, 1) if h else queries
    at = lane(q.shape)
    return jnp.where(at < FEATURE_WIDTH, q * FEATURE_WIDTH**-0.5, 0.0), at == FEATURE_WIDTH


def weigh(scores, keep=None):
    weight = scores * scores + 1.0
    if keep is not None:
        weight = jnp.where(keep, weight, 0.0)
    return weight.astype(BF16)


def divide(total, mask):
    below = jnp.broadcast_to(total[:, 0:1], total.shape) + 2.0 * (1.0 - mask)
    return mask * total / below


def emit(att, o_ref, first_ref, rest, tail_rows):
    place = gray(lax.axis_index("col"))
    for s in range(4):
        part = dot(att, o_ref[gray((place + 3 - s) & 3)])
        out = first_ref if s == 0 else rest[s - 1]
        for t in range(3):
            out[t * HALF : (t + 1) * HALF, :] = part[:HALF, t * 128 : (t + 1) * 128].astype(out.dtype)
        last = part[:, 384:512]
        middle = lane((HALF // 2, 128)) < 64
        out[TAIL:BODY, :] = jnp.where(middle, last[: HALF // 2], last[HALF // 2 : HALF]).astype(out.dtype)
        if tail_rows:
            for t in range(4):
                out[BODY + 8 * t : BODY + 8 * t + 8, :] = part[
                    HALF : HALF + 8, t * 128 : (t + 1) * 128
                ].astype(out.dtype)


def chunk_a(a0, a1, a2, a3, w_ref, o_ref, ck_ref, cv_ref, m_ref, first, r1, r2, r3, ka_ref, va_ref):
    blocks = (a0, a1, a2, a3)
    kv, queries = project(blocks, blocks, w_ref, HALF)
    mask = m_ref[0:HALF, :]
    ka_ref[...] = as_keys(kv)
    va_ref[...] = as_values(kv, jnp.concatenate([mask] * 4, axis=1) > 0.0)
    causal = lane((HALF, HALF)) <= row((HALF, HALF))
    outs = []
    for h in range(4):
        at = slice(h * LANES, (h + 1) * LANES)
        q, one = query_of(queries, h)
        q = jnp.where(one, 1.0, q).astype(BF16)
        total = dot(weigh(dot_nt(q, ka_ref[:, at]), causal), va_ref[:, at])
        for b in range(2):
            keys = slice(b * 512, (b + 1) * 512)
            total += dot(weigh(dot_nt(q, ck_ref[keys, at])), cv_ref[keys, at])
        outs.append(divide(total, mask).astype(BF16))
    emit(jnp.concatenate(outs, axis=1), o_ref, first, (r1, r2, r3), False)


def chunk_b(
    b0, b1, b2, b3, a0, a1, a2, a3, w_ref, o_ref, ck_ref, cv_ref, m_ref, ka_ref, va_ref, len_ref, cache,
    first, r1, r2, r3, kb, vb, slab, sems,
):
    copies = [pltpu.make_async_copy(cache.at[d + 1], slab.at[d], sems.at[d]) for d in range(DEC)]
    for copy in copies:
        copy.start()
    rows = HALF + 16
    kv, queries = project((b0, b1, b2, b3), (a0, a1, a2, a3), w_ref, rows)
    mask = m_ref[HALF : 2 * HALF, :]
    kb[...] = as_keys(kv[:HALF])
    vb[...] = as_values(kv[:HALF], jnp.concatenate([mask] * 4, axis=1) > 0.0)
    causal = lane((HALF, HALF)) <= row((HALF, HALF))
    outs, late = [], []
    for h in range(4):
        at = slice(h * LANES, (h + 1) * LANES)
        q, one = query_of(queries, h)
        late.append(q[HALF:])
        q = jnp.where(one, 1.0, q)[:HALF].astype(BF16)
        total = dot(weigh(dot_nt(q, kb[:, at]), causal), vb[:, at])
        total += dot(weigh(dot_nt(q, ka_ref[:, at])), va_ref[:, at])
        for b in range(2):
            keys = slice(b * 512, (b + 1) * 512)
            total += dot(weigh(dot_nt(q, ck_ref[keys, at])), cv_ref[keys, at])
        outs.append(divide(total, mask))
    late = jnp.concatenate(late, axis=1)
    fresh = kv[HALF:]
    own = row((16, 512)) == lane((16, 512)) // LANES
    position = lane((16, 1024))
    decoded = jnp.zeros((16, 512), F32)
    for d in range(DEC):
        copies[d].wait()
        q = jnp.where(own, jnp.broadcast_to(late[d : d + 1], (16, 512)), 0.0)
        new = jnp.broadcast_to(fresh[d : d + 1], (16, 512))
        live = m_ref[2 * HALF + d : 2 * HALF + d + 1, 0:1]
        score = dot_nt(q.astype(BF16), slab[d]) + 1.0
        weight = jnp.where(position < len_ref[d + 1], score * score + 1.0, 0.0)
        self_score = jnp.sum(q * new, axis=1, keepdims=True) + 1.0
        self_weight = (self_score * self_score + 1.0) * live
        total = dot(weight.astype(BF16), slab[d]) + self_weight.astype(BF16).astype(F32) * new
        below = jnp.sum(weight, axis=1, keepdims=True) + self_weight + 2.0 * (1.0 - live)
        value = jnp.sum(jnp.where(own, live * total / below, 0.0), axis=0, keepdims=True)
        decoded = jnp.where(row((16, 512)) == d, jnp.broadcast_to(value, (16, 512)), decoded)
    att = jnp.concatenate([jnp.concatenate(outs, axis=1), decoded], axis=0).astype(BF16)
    emit(att, o_ref, first, (r1, r2, r3), True)


def finish(ra, pa, rb, pb, out):
    for recv, part, base in ((ra, pa, 0), (rb, pb, HALF)):
        for t in range(3):
            at = slice(t * HALF, (t + 1) * HALF)
            out[base : base + HALF, t * 128 : (t + 1) * 128] = (
                recv[at, :].astype(F32) + part[at, :]
            ).astype(BF16)
        tail = recv[TAIL:BODY, :].astype(F32) + part[TAIL:BODY, :]
        out[base : base + HALF // 2, 384:448] = tail[:, 0:64].astype(BF16)
        out[base + HALF // 2 : base + HALF, 384:448] = tail[:, 64:128].astype(BF16)
    for t in range(4):
        at = slice(BODY + 8 * t, BODY + 8 * t + DEC)
        width = 128 if t < 3 else 64
        late = (rb[at, :].astype(F32) + pb[at, :])[:, 0:width]
        out[SPAN_TOKENS:, t * 128 : t * 128 + width] = late.astype(BF16)


def shards(hidden, norm_gain, qkv_weight, out_weight, cache, cached, token_mask):
    ring = [(gray(p), gray((p + 1) % 4)) for p in range(4)]

    def onward(x):
        return lax.ppermute(x, "col", ring)

    def across(x, k):
        return lax.ppermute(x, "row", [(i, i ^ k) for i in range(8)])

    a, b = call(
        pack_tokens,
        (shaped((BODY + EXTRA, 128)), shaped((BODY + EXTRA, 128))),
        [VMEM, VMEM],
        nbytes=2_000_000,
        name="pack_tokens",
    )(hidden, norm_gain.reshape(1, -1))
    a, b = [a], [b]
    a.append(onward(a[-1]))
    b.append(onward(b[-1]))
    own = call(pack_weights, shaped((5 * QROWS + 2 * OROWS, 128)), [VMEM, VMEM], nbytes=2_000_000, name="pack_weights")(
        qkv_weight, out_weight
    )
    plane = [own, across(own, 2), across(own, 4), across(own, 6)]
    for _ in range(2):
        a.append(onward(a[-1]))
        b.append(onward(b[-1]))
    blocks = []
    for block in plane:
        blocks += [block, across(block, 1)]
    w, o = call(
        place_weights,
        (shaped((4, 512, 640)), shaped((4, 512, 512))),
        [VMEM] * 8,
        nbytes=8_000_000,
        name="place_weights",
    )(*blocks)
    ck, cv = call(
        prepare_cache,
        (shaped((1024, 512)), shaped((1024, 512))),
        [ANY, SMEM],
        scratch=[pltpu.VMEM((1024, 512), BF16), pltpu.SemaphoreType.DMA],
        nbytes=3_000_000,
        name="prepare_cache",
    )(cache, cached)
    mask = jnp.broadcast_to(token_mask.astype(F32)[:, None], (token_mask.shape[0], 128))
    body = shaped((BODY, 128), F32)
    first, *rest_a, ka, va = call(
        chunk_a,
        (shaped((BODY, 128)), body, body, body, shaped((HALF, 512)), shaped((HALF, 512))),
        [VMEM] * 9,
        flops=4_000_000_000,
        nbytes=12_000_000,
        name="chunk_a",
    )(*a, w, o, ck, cv, mask)
    send_a = onward(first)
    body = shaped((BODY + EXTRA, 128), F32)
    first, *rest_b = call(
        chunk_b,
        (shaped((BODY + EXTRA, 128)), body, body, body),
        [VMEM] * 15 + [SMEM, ANY],
        scratch=[
            pltpu.VMEM((HALF, 512), BF16),
            pltpu.VMEM((HALF, 512), BF16),
            pltpu.VMEM((DEC, 1024, 512), BF16),
            pltpu.SemaphoreType.DMA((DEC,)),
        ],
        flops=5_000_000_000,
        nbytes=16_000_000,
        name="chunk_b",
    )(*b, *a, w, o, ck, cv, mask, ka, va, cached, cache)
    send_b = onward(first)
    for s in range(2):
        send_a = onward((send_a.astype(F32) + rest_a[s]).astype(BF16))
        send_b = onward((send_b.astype(F32) + rest_b[s]).astype(BF16))
    return call(finish, shaped(hidden.shape), [VMEM] * 4, nbytes=3_000_000, name="finish")(
        send_a, rest_a[2], send_b, rest_b[2]
    )


def taylor(taylor_score):
    return 1.0 + taylor_score + 0.5 * taylor_score * taylor_score


def attend(projected, cache, cached, token_mask):
    rows = projected.shape[0]
    width = 2 * FEATURE_WIDTH + HDIM
    lanes = FEATURE_WIDTH + HDIM
    heads_here = projected.shape[1] // width
    parts = projected.reshape(rows, heads_here, width)
    query_rows = parts[:, :, :FEATURE_WIDTH]
    key_rows = parts[:, :, FEATURE_WIDTH : 2 * FEATURE_WIDTH]
    values = parts[:, :, 2 * FEATURE_WIDTH :]
    store = cache.reshape(cache.shape[0], cache.shape[1], heads_here, lanes)
    capacity = cache.shape[1]
    block = min(512, capacity)
    score_scale = FEATURE_WIDTH ** (-0.5)
    live = token_mask.astype(jnp.float32)
    prefill_query_rows = query_rows[:SPAN_TOKENS]
    prior_tokens = store[0]
    offset = cached[0]

    def span_step(index, carry):
        numer, denom = carry
        span_slice = lax.dynamic_slice_in_dim(prior_tokens, index * block, block, 0)
        position = index * block + lax.iota(jnp.int32, block)
        taylor_score = (
            jnp.einsum(
                "sue,pue->usp",
                prefill_query_rows,
                span_slice[:, :, :FEATURE_WIDTH],
                preferred_element_type=jnp.float32,
            )
            * score_scale
        )
        weight = taylor(taylor_score) * (position < offset).astype(jnp.float32)[None, None, :]
        numer = numer + jnp.einsum(
            "hqk,khd->hqd",
            weight.astype(jnp.bfloat16),
            span_slice[:, :, FEATURE_WIDTH:],
            preferred_element_type=jnp.float32,
        )
        return (numer, denom + jnp.sum(weight, axis=-1))

    start_numer = jnp.zeros((heads_here, SPAN_TOKENS, HDIM), jnp.float32)
    start_denom = jnp.zeros((heads_here, SPAN_TOKENS), jnp.float32)
    span_blocks = (offset + block - 1) // block
    numer, denom = lax.fori_loop(0, span_blocks, span_step, (start_numer, start_denom))
    taylor_score = (
        jnp.einsum(
            "sue,pue->usp",
            prefill_query_rows,
            key_rows[:SPAN_TOKENS],
            preferred_element_type=jnp.float32,
        )
        * score_scale
    )
    order = lax.iota(jnp.int32, SPAN_TOKENS)
    allowed = (order[None, :] <= order[:, None]).astype(jnp.float32) * live[:SPAN_TOKENS][None, :]
    weight = taylor(taylor_score) * allowed[None]
    numer = numer + jnp.einsum(
        "hqk,khd->hqd",
        weight.astype(jnp.bfloat16),
        values[:SPAN_TOKENS],
        preferred_element_type=jnp.float32,
    )
    denom = denom + jnp.sum(weight, axis=-1)
    decode_queries = query_rows[SPAN_TOKENS:]
    past = store[1:]
    counts = cached[1:]

    def decode_step(index, carry):
        dec_numer, dec_denom = carry
        span_slice = lax.dynamic_slice_in_dim(past, index * block, block, 1)
        position = index * block + lax.iota(jnp.int32, block)
        taylor_score = (
            jnp.einsum(
                "rhf,rkhf->rhk",
                decode_queries,
                span_slice[..., :FEATURE_WIDTH],
                preferred_element_type=jnp.float32,
            )
            * score_scale
        )
        seen = (position[None, :] < counts[:, None]).astype(jnp.float32)
        weight = taylor(taylor_score) * seen[:, None, :]
        dec_numer = dec_numer + jnp.einsum(
            "rhk,rkhd->rhd",
            weight.astype(jnp.bfloat16),
            span_slice[..., FEATURE_WIDTH:],
            preferred_element_type=jnp.float32,
        )
        return (dec_numer, dec_denom + jnp.sum(weight, axis=-1))

    first_numer = jnp.zeros((DEC, heads_here, HDIM), jnp.float32)
    first_denom = jnp.zeros((DEC, heads_here), jnp.float32)
    decode_blocks = (jnp.max(counts) + block - 1) // block
    dec_numer, dec_denom = lax.fori_loop(0, decode_blocks, decode_step, (first_numer, first_denom))
    taylor_score = (
        jnp.sum(
            decode_queries.astype(jnp.float32) * key_rows[SPAN_TOKENS:].astype(jnp.float32), axis=-1
        )
        * score_scale
    )
    weight = taylor(taylor_score) * live[SPAN_TOKENS:, None]
    dec_numer = dec_numer + weight.astype(jnp.bfloat16).astype(jnp.float32)[..., None] * values[
        SPAN_TOKENS:
    ].astype(jnp.float32)
    dec_denom = dec_denom + weight
    numer_all = jnp.concatenate([jnp.transpose(numer, (1, 0, 2)), dec_numer], axis=0)
    denom_all = jnp.concatenate([jnp.transpose(denom, (1, 0)), dec_denom], axis=0)
    result = live[:, None, None] * numer_all / (denom_all + 1.0 - live[:, None])[..., None]
    return result.astype(jnp.bfloat16).reshape(rows, heads_here * HDIM)


def plain_shards(hidden, norm_gain, qkv_weight, out_weight, cache, cached, token_mask):
    full, gain = (
        lax.all_gather(hidden, "col", axis=1, tiled=True),
        lax.all_gather(norm_gain, "col", axis=0, tiled=True),
    )
    wide = full.astype(jnp.float32)
    normed = (
        wide
        * lax.rsqrt(jnp.mean(wide * wide, axis=-1, keepdims=True) + 1e-06)
        * gain.astype(jnp.float32)
    )
    normed = normed.astype(jnp.bfloat16)
    projected = jnp.dot(
        normed,
        lax.all_gather(qkv_weight, "row", axis=0, tiled=True),
        preferred_element_type=jnp.float32,
    ).astype(jnp.bfloat16)
    attended = attend(projected, cache, cached, token_mask)
    terms = jnp.dot(
        attended,
        lax.all_gather(out_weight, "row", axis=1, tiled=True),
        preferred_element_type=jnp.float32,
    )
    mixed = lax.psum_scatter(terms, "col", scatter_dimension=1, tiled=True).astype(jnp.bfloat16)
    return mixed


def solution(mesh):
    in_specs = (
        P("row", "col"),
        P("col"),
        P("row", "col"),
        P("col", "row"),
        P("row", None, "col"),
        P("row"),
        P("row"),
    )
    out_specs = P("row", "col")
    body = shards if (mesh.shape["row"], mesh.shape["col"]) == (8, 4) else plain_shards
    return jax.shard_map(body, mesh=mesh, in_specs=in_specs, out_specs=out_specs, check_vma=False)
```

```python
import jax
import jax.numpy as jnp
from jax import lax
from jax.experimental import pallas as pl
from jax.experimental.pallas import tpu as pltpu
from jax.sharding import PartitionSpec as P

FEATURE_WIDTH = 16
HDIM = 112
SPAN_TOKENS = 512
DEC = 4
LANES = FEATURE_WIDTH + HDIM
F32 = jnp.float32
BF16 = jnp.bfloat16
HALF = SPAN_TOKENS // 2
VMEM = pl.BlockSpec(memory_space=pltpu.VMEM)
SMEM = pl.BlockSpec(memory_space=pltpu.SMEM)
HBM = pl.BlockSpec(memory_space=pltpu.MemorySpace.HBM)
TAIL = 3 * HALF
BODY = TAIL + HALF // 2
EXTRA = 32
QROWS = 224
OROWS = 448
WROWS = 4 * QROWS + 2 * OROWS


def gray(place):
    return place ^ (place >> 1)


def call(body, outs, in_specs, scratch=(), flops=0, nbytes=0, name=None, mib=8):
    return pl.pallas_call(
        body,
        out_shape=outs,
        in_specs=in_specs,
        out_specs=jax.tree.map(lambda _: VMEM, outs),
        scratch_shapes=scratch,
        cost_estimate=pl.CostEstimate(flops=flops, bytes_accessed=nbytes, transcendentals=0),
        compiler_params=pltpu.CompilerParams(vmem_limit_bytes=mib * 1024 * 1024),
        name=name,
    )


def shaped(shape, dtype=BF16):
    return jax.ShapeDtypeStruct(shape, dtype)


def dot(a, b):
    return jnp.dot(a, b, preferred_element_type=F32)


def dot_nt(a, b):
    return lax.dot_general(a, b, (((1,), (1,)), ((), ())), preferred_element_type=F32)


def lane(shape):
    return lax.broadcasted_iota(jnp.int32, shape, len(shape) - 1)


def row(shape):
    return lax.broadcasted_iota(jnp.int32, shape, 0)


def pack(hidden, gains, qkv, outs, a_ref, b_ref, w_ref, h_ref, g_ref, q_ref, o_ref, sems):
    pairs = ((hidden, h_ref), (gains, g_ref), (qkv, q_ref), (outs, o_ref))
    copies = [pltpu.make_async_copy(*pair, sems.at[n]) for n, pair in enumerate(pairs)]
    for copy in copies:
        copy.start()
    copies[0].wait()
    copies[1].wait()
    for ref, base in ((a_ref, 0), (b_ref, HALF)):
        for t in range(3):
            ref[t * HALF : (t + 1) * HALF, :] = h_ref[base : base + HALF, t * 128 : (t + 1) * 128]
        low = h_ref[base : base + HALF // 2, 384:448]
        high = h_ref[base + HALF // 2 : base + HALF, 384:448]
        ref[TAIL:BODY, :] = jnp.concatenate([low, high], axis=1)
        ref[BODY:, :] = jnp.zeros((EXTRA, 128), BF16)
    gain = g_ref[...].reshape(1, 448)
    for t in range(3):
        a_ref[BODY + 8 * t : BODY + 8 * t + 1, :] = gain[:, t * 128 : (t + 1) * 128]
        b_ref[BODY + 8 * t : BODY + 8 * t + DEC, :] = h_ref[SPAN_TOKENS:, t * 128 : (t + 1) * 128]
    last = gain[:, 384:448]
    a_ref[BODY + 24 : BODY + 25, :] = jnp.concatenate([last, last], axis=1)
    b_ref[BODY + 24 : BODY + 24 + DEC, 0:64] = h_ref[SPAN_TOKENS:, 384:448]
    copies[2].wait()
    copies[3].wait()
    width = FEATURE_WIDTH + LANES
    for h in range(4):
        w_ref[h * QROWS : (h + 1) * QROWS, :] = q_ref[:, h * width + FEATURE_WIDTH : (h + 1) * width]
    at = 4 * QROWS
    w_ref[at : at + OROWS, :] = o_ref[:, 0:128]
    for side in range(2):
        pieces = [o_ref[side * QROWS : (side + 1) * QROWS, 128:224]]
        for h in (2 * side, 2 * side + 1):
            pieces.append(q_ref[:, h * width : h * width + FEATURE_WIDTH])
        rows = at + OROWS + side * QROWS
        w_ref[rows : rows + QROWS, :] = jnp.concatenate(pieces, axis=1)


def place_weights(*refs):
    blocks, (w_ref, o_ref) = refs[:8], refs[8:]
    me = lax.axis_index("row")
    at, late = 4 * QROWS, 4 * QROWS + OROWS

    def project_rows(block):
        queries = [block[late + s * QROWS : late + (s + 1) * QROWS, 96:128] for s in range(2)]
        queries.append(jnp.zeros((QROWS, 64), BF16))
        heads = [block[h * QROWS : (h + 1) * QROWS, :] for h in range(4)]
        return heads + [jnp.concatenate(queries, axis=1)]

    for core in range(2):

        @pl.when(me & 1 == core)
        def _():
            for k in range(4):
                j = (me >> 1) ^ k
                low, high = blocks[2 * k + core], blocks[2 * k + 1 - core]
                for t, tile in enumerate(project_rows(low)):
                    w_ref[j, 0:QROWS, t * 128 : (t + 1) * 128] = tile
                for t, tile in enumerate(project_rows(high)):
                    w_ref[j, QROWS : 2 * QROWS, t * 128 : (t + 1) * 128] = tile
                    w_ref[j, 448:512, t * 128 : (t + 1) * 128] = tile[160:QROWS, :]
                full = jnp.concatenate(
                    [low[at:late, :], low[late:, 0:96], high[at:late, :], high[late:, 0:96]], axis=1
                )
                full = jnp.concatenate([full, full[:, 384:448]], axis=1)
                for h in range(4):
                    o_ref[j, h * LANES : h * LANES + FEATURE_WIDTH, :] = jnp.zeros((FEATURE_WIDTH, 512), BF16)
                    o_ref[j, h * LANES + FEATURE_WIDTH : (h + 1) * LANES, :] = full[h * HDIM : (h + 1) * HDIM, :]


def as_keys(kv):
    return jnp.where(lane(kv.shape) % LANES == FEATURE_WIDTH, 1.0, kv).astype(BF16)


def as_values(kv, keep):
    ones = jnp.where(lane(kv.shape) % LANES < FEATURE_WIDTH, 1.0, kv)
    return jnp.where(keep, ones, 0.0).astype(BF16)


def prepare_cache(cache, len_ref, k_ref, v_ref, slab, sem):
    copy = pltpu.make_async_copy(cache.at[0], slab, sem)
    copy.start()
    copy.wait()
    kv = slab[...].astype(F32)
    k_ref[...] = as_keys(kv)
    v_ref[...] = as_values(kv, row(kv.shape) < len_ref[0])


def norm(blocks, gain_ref, out_ref, rows):
    middle = lane((HALF // 2, 128)) < 64
    pieces, square = [], None
    for ref in blocks:
        tail = ref[TAIL:BODY, :].astype(F32)
        tail = jnp.concatenate([jnp.where(middle, tail, 0.0), jnp.where(middle, 0.0, tail)], axis=0)
        tiles = [ref[t * HALF : (t + 1) * HALF, :].astype(F32) for t in range(3)] + [tail]
        if rows > HALF:
            tiles = [
                jnp.concatenate(
                    [
                        tile,
                        ref[BODY + 8 * t : BODY + 8 * t + 8, :].astype(F32),
                        jnp.zeros((8, 128), F32),
                    ],
                    axis=0,
                )
                for t, tile in enumerate(tiles)
            ]
        pieces.append(tiles)
        for tile in tiles:
            square = tile * tile if square is None else square + tile * tile
    mean = jnp.sum(square, axis=1, keepdims=True) * (1.0 / 1792.0)
    scale = jnp.broadcast_to(lax.rsqrt(mean + 1e-06), (rows, 128))
    for k, tiles in enumerate(pieces):
        for t, tile in enumerate(tiles):
            gain = gain_ref[k][BODY + 8 * t : BODY + 8 * t + 1, :].astype(F32)
            out_ref[:, k * 512 + t * 128 : k * 512 + (t + 1) * 128] = (tile * scale * gain).astype(BF16)


def norm_a(a0, a1, a2, a3, out):
    norm((a0, a1, a2, a3), (a0, a1, a2, a3), out, HALF)


def norm_b(b0, b1, b2, b3, a0, a1, a2, a3, out):
    norm((b0, b1, b2, b3), (a0, a1, a2, a3), out, HALF + 16)


def project(normed, w_ref):
    place = gray(lax.axis_index("col"))
    total = None
    for k in range(4):
        term = dot(normed[:, k * 512 : (k + 1) * 512], w_ref[gray((place + 4 - k) & 3)])
        total = term if total is None else total + term
    total = total.astype(BF16).astype(F32)
    return total[:, 0:512], total[:, 512:640]


def query_of(queries, h):
    q = pltpu.roll(queries, (128 - FEATURE_WIDTH * h) % 128, 1) if h else queries
    at = lane(q.shape)
    return jnp.where(at < FEATURE_WIDTH, q * FEATURE_WIDTH**-0.5, 0.0), at == FEATURE_WIDTH


def weigh(scores, keep=None):
    weight = scores * scores + 1.0
    if keep is not None:
        weight = jnp.where(keep, weight, 0.0)
    return weight.astype(BF16)


def divide(total, mask):
    below = jnp.broadcast_to(total[:, 0:1], total.shape) + 2.0 * (1.0 - mask)
    return mask * total / below


def emit(att, o_ref, first_ref, rest, tail_rows):
    place = gray(lax.axis_index("col"))
    for s in range(4):
        part = dot(att, o_ref[gray((place + 3 - s) & 3)])
        out = first_ref if s == 0 else rest[s - 1]
        for t in range(3):
            out[t * HALF : (t + 1) * HALF, :] = part[:HALF, t * 128 : (t + 1) * 128].astype(out.dtype)
        last = part[:, 384:512]
        middle = lane((HALF // 2, 128)) < 64
        out[TAIL:BODY, :] = jnp.where(middle, last[: HALF // 2], last[HALF // 2 : HALF]).astype(out.dtype)
        if tail_rows:
            for t in range(4):
                out[BODY + 8 * t : BODY + 8 * t + 8, :] = part[
                    HALF : HALF + 8, t * 128 : (t + 1) * 128
                ].astype(out.dtype)


def chunk_a(normed, w_ref, o_ref, ck_ref, cv_ref, m_ref, first, r1, r2, r3, ka_ref, va_ref):
    kv, queries = project(normed, w_ref)
    mask = m_ref[0:HALF, :]
    ka_ref[...] = as_keys(kv)
    va_ref[...] = as_values(kv, jnp.concatenate([mask] * 4, axis=1) > 0.0)
    causal = lane((HALF, HALF)) <= row((HALF, HALF))
    outs = []
    for h in range(4):
        at = slice(h * LANES, (h + 1) * LANES)
        q, one = query_of(queries, h)
        q = jnp.where(one, 1.0, q).astype(BF16)
        total = dot(weigh(dot_nt(q, ka_ref[:, at]), causal), va_ref[:, at])
        for b in range(2):
            keys = slice(b * 512, (b + 1) * 512)
            total += dot(weigh(dot_nt(q, ck_ref[keys, at])), cv_ref[keys, at])
        outs.append(divide(total, mask).astype(BF16))
    emit(jnp.concatenate(outs, axis=1), o_ref, first, (r1, r2, r3), False)


def chunk_b(
    normed, w_ref, ck_ref, cv_ref, m_ref, ka_ref, va_ref, len_ref, cache,
    att_ref, kb, vb, slab, sems,
):
    copies = [pltpu.make_async_copy(cache.at[d + 1], slab.at[d], sems.at[d]) for d in range(DEC)]
    for copy in copies:
        copy.start()
    kv, queries = project(normed, w_ref)
    mask = m_ref[HALF : 2 * HALF, :]
    kb[...] = as_keys(kv[:HALF])
    vb[...] = as_values(kv[:HALF], jnp.concatenate([mask] * 4, axis=1) > 0.0)
    causal = lane((HALF, HALF)) <= row((HALF, HALF))
    outs, late = [], []
    for h in range(4):
        at = slice(h * LANES, (h + 1) * LANES)
        q, one = query_of(queries, h)
        late.append(q[HALF:])
        q = jnp.where(one, 1.0, q)[:HALF].astype(BF16)
        total = dot(weigh(dot_nt(q, kb[:, at]), causal), vb[:, at])
        total += dot(weigh(dot_nt(q, ka_ref[:, at])), va_ref[:, at])
        for b in range(2):
            keys = slice(b * 512, (b + 1) * 512)
            total += dot(weigh(dot_nt(q, ck_ref[keys, at])), cv_ref[keys, at])
        outs.append(divide(total, mask))
    late = jnp.concatenate(late, axis=1)
    fresh = kv[HALF:]
    own = row((16, 512)) == lane((16, 512)) // LANES
    position = lane((16, 1024))
    decoded = jnp.zeros((16, 512), F32)
    for d in range(DEC):
        copies[d].wait()
        q = jnp.where(own, jnp.broadcast_to(late[d : d + 1], (16, 512)), 0.0)
        new = jnp.broadcast_to(fresh[d : d + 1], (16, 512))
        live = m_ref[2 * HALF + d : 2 * HALF + d + 1, 0:1]
        score = dot_nt(q.astype(BF16), slab[d]) + 1.0
        weight = jnp.where(position < len_ref[d + 1], score * score + 1.0, 0.0)
        self_score = jnp.sum(q * new, axis=1, keepdims=True) + 1.0
        self_weight = (self_score * self_score + 1.0) * live
        total = dot(weight.astype(BF16), slab[d]) + self_weight.astype(BF16).astype(F32) * new
        below = jnp.sum(weight, axis=1, keepdims=True) + self_weight + 2.0 * (1.0 - live)
        value = jnp.sum(jnp.where(own, live * total / below, 0.0), axis=0, keepdims=True)
        decoded = jnp.where(row((16, 512)) == d, jnp.broadcast_to(value, (16, 512)), decoded)
    att_ref[:HALF, :] = jnp.concatenate(outs, axis=1).astype(BF16)
    att_ref[HALF:, :] = decoded.astype(BF16)


def emit_b(att_ref, o_ref, first, r1, r2, r3):
    emit(att_ref[...], o_ref, first, (r1, r2, r3), True)


def finish(ra, pa, rb, pb, out):
    for recv, part, base in ((ra, pa, 0), (rb, pb, HALF)):
        for t in range(3):
            at = slice(t * HALF, (t + 1) * HALF)
            out[base : base + HALF, t * 128 : (t + 1) * 128] = (
                recv[at, :].astype(F32) + part[at, :]
            ).astype(BF16)
        tail = recv[TAIL:BODY, :].astype(F32) + part[TAIL:BODY, :]
        out[base : base + HALF // 2, 384:448] = tail[:, 0:64].astype(BF16)
        out[base + HALF // 2 : base + HALF, 384:448] = tail[:, 64:128].astype(BF16)
    for t in range(4):
        at = slice(BODY + 8 * t, BODY + 8 * t + DEC)
        width = 128 if t < 3 else 64
        late = (rb[at, :].astype(F32) + pb[at, :])[:, 0:width]
        out[SPAN_TOKENS:, t * 128 : t * 128 + width] = late.astype(BF16)


def in_hbm(x):
    return pltpu.with_memory_space_constraint(x, pltpu.MemorySpace.HBM)


def after(value, *others):
    return lax.optimization_barrier((value, *others))[0]


def shards(hidden, norm_gain, qkv_weight, out_weight, cache, cached, token_mask):
    ring = [(gray(p), gray((p + 1) % 4)) for p in range(4)]

    def onward(x):
        return lax.ppermute(x, "col", ring)

    def across(x, k):
        return lax.ppermute(x, "row", [(i, i ^ k) for i in range(8)])

    a, b, own = call(
        pack,
        (shaped((BODY + EXTRA, 128)), shaped((BODY + EXTRA, 128)), shaped((WROWS, 128))),
        [HBM] * 4,
        scratch=[pltpu.VMEM(x.shape, BF16) for x in (hidden, norm_gain, qkv_weight, out_weight)]
        + [pltpu.SemaphoreType.DMA((4,))],
        nbytes=300_000,
        name="pack",
    )(*(in_hbm(x) for x in (hidden, norm_gain, qkv_weight, out_weight)))
    a, b = [a], [b]
    for _ in range(3):
        b.append(onward(b[-1]))
        a.append(onward(a[-1]))
    plane = [own] + [across(own, k) for k in (2, 4, 6)]
    blocks = [own, across(after(own, a[2], b[2]), 1)]
    for block in plane[1:]:
        blocks += [block, across(block, 1)]
    w, o = call(
        place_weights,
        (shaped((4, 512, 640)), shaped((4, 512, 512))),
        [VMEM] * 8,
        nbytes=300_000,
        name="place_weights",
    )(*blocks)
    a[3] = after(a[3], w)
    na = call(norm_a, shaped((HALF, 2048)), [VMEM] * 4, nbytes=30_000_000, name="norm_a")(*a)
    nb = call(norm_b, shaped((HALF + 16, 2048)), [VMEM] * 8, nbytes=300_000, name="norm_b")(*b, *a)
    ck, cv = call(
        prepare_cache,
        (shaped((1024, 512)), shaped((1024, 512))),
        [HBM, SMEM],
        scratch=[pltpu.VMEM((1024, 512), BF16), pltpu.SemaphoreType.DMA],
        nbytes=300_000,
        name="prepare_cache",
        mib=12,
    )(in_hbm(cache), cached)
    mask = jnp.broadcast_to(token_mask.astype(F32)[:, None], (token_mask.shape[0], 128))
    body = shaped((BODY, 128), F32)
    first, *rest_a, ka, va = call(
        chunk_a,
        (shaped((BODY, 128)), body, body, body, shaped((HALF, 512)), shaped((HALF, 512))),
        [VMEM] * 6,
        flops=100_000_000,
        nbytes=300_000,
        name="chunk_a",
        mib=20,
    )(na, w, o, ck, cv, mask)
    send_a = onward(first)
    att = call(
        chunk_b,
        shaped((HALF + 16, 512)),
        [VMEM] * 7 + [SMEM, HBM],
        scratch=[
            pltpu.VMEM((HALF, 512), BF16),
            pltpu.VMEM((HALF, 512), BF16),
            pltpu.VMEM((DEC, 1024, 512), BF16),
            pltpu.SemaphoreType.DMA((DEC,)),
        ],
        flops=100_000_000,
        nbytes=300_000,
        name="chunk_b",
        mib=20,
    )(nb, w, ck, cv, mask, ka, va, cached, in_hbm(cache))
    arrived = send_a
    body = shaped((BODY + EXTRA, 128), F32)
    first, *rest_b = call(
        emit_b,
        (shaped((BODY + EXTRA, 128)), body, body, body),
        [VMEM] * 2,
        flops=600_000_000,
        nbytes=4_000_000,
        name="emit_b",
    )(after(att, arrived), o)
    send_b = onward(first)
    send_a = onward((arrived.astype(F32) + rest_a[0]).astype(BF16))
    send_b = onward((after(send_b, send_a).astype(F32) + rest_b[0]).astype(BF16))
    send_a = onward((send_a.astype(F32) + rest_a[1]).astype(BF16))
    send_b = onward((after(send_b, send_a).astype(F32) + rest_b[1]).astype(BF16))
    return call(finish, shaped(hidden.shape), [VMEM] * 4, nbytes=300_000, name="finish")(
        send_a, rest_a[2], send_b, rest_b[2]
    )


def taylor(taylor_score):
    return 1.0 + taylor_score + 0.5 * taylor_score * taylor_score


def attend(projected, cache, cached, token_mask):
    rows = projected.shape[0]
    width = 2 * FEATURE_WIDTH + HDIM
    lanes = FEATURE_WIDTH + HDIM
    heads_here = projected.shape[1] // width
    parts = projected.reshape(rows, heads_here, width)
    query_rows = parts[:, :, :FEATURE_WIDTH]
    key_rows = parts[:, :, FEATURE_WIDTH : 2 * FEATURE_WIDTH]
    values = parts[:, :, 2 * FEATURE_WIDTH :]
    store = cache.reshape(cache.shape[0], cache.shape[1], heads_here, lanes)
    capacity = cache.shape[1]
    block = min(512, capacity)
    score_scale = FEATURE_WIDTH ** (-0.5)
    live = token_mask.astype(jnp.float32)
    prefill_query_rows = query_rows[:SPAN_TOKENS]
    prior_tokens = store[0]
    offset = cached[0]

    def span_step(index, carry):
        numer, denom = carry
        span_slice = lax.dynamic_slice_in_dim(prior_tokens, index * block, block, 0)
        position = index * block + lax.iota(jnp.int32, block)
        taylor_score = (
            jnp.einsum(
                "sue,pue->usp",
                prefill_query_rows,
                span_slice[:, :, :FEATURE_WIDTH],
                preferred_element_type=jnp.float32,
            )
            * score_scale
        )
        weight = taylor(taylor_score) * (position < offset).astype(jnp.float32)[None, None, :]
        numer = numer + jnp.einsum(
            "hqk,khd->hqd",
            weight.astype(jnp.bfloat16),
            span_slice[:, :, FEATURE_WIDTH:],
            preferred_element_type=jnp.float32,
        )
        return (numer, denom + jnp.sum(weight, axis=-1))

    start_numer = jnp.zeros((heads_here, SPAN_TOKENS, HDIM), jnp.float32)
    start_denom = jnp.zeros((heads_here, SPAN_TOKENS), jnp.float32)
    span_blocks = (offset + block - 1) // block
    numer, denom = lax.fori_loop(0, span_blocks, span_step, (start_numer, start_denom))
    taylor_score = (
        jnp.einsum(
            "sue,pue->usp",
            prefill_query_rows,
            key_rows[:SPAN_TOKENS],
            preferred_element_type=jnp.float32,
        )
        * score_scale
    )
    order = lax.iota(jnp.int32, SPAN_TOKENS)
    allowed = (order[None, :] <= order[:, None]).astype(jnp.float32) * live[:SPAN_TOKENS][None, :]
    weight = taylor(taylor_score) * allowed[None]
    numer = numer + jnp.einsum(
        "hqk,khd->hqd",
        weight.astype(jnp.bfloat16),
        values[:SPAN_TOKENS],
        preferred_element_type=jnp.float32,
    )
    denom = denom + jnp.sum(weight, axis=-1)
    decode_queries = query_rows[SPAN_TOKENS:]
    past = store[1:]
    counts = cached[1:]

    def decode_step(index, carry):
        dec_numer, dec_denom = carry
        span_slice = lax.dynamic_slice_in_dim(past, index * block, block, 1)
        position = index * block + lax.iota(jnp.int32, block)
        taylor_score = (
            jnp.einsum(
                "rhf,rkhf->rhk",
                decode_queries,
                span_slice[..., :FEATURE_WIDTH],
                preferred_element_type=jnp.float32,
            )
            * score_scale
        )
        seen = (position[None, :] < counts[:, None]).astype(jnp.float32)
        weight = taylor(taylor_score) * seen[:, None, :]
        dec_numer = dec_numer + jnp.einsum(
            "rhk,rkhd->rhd",
            weight.astype(jnp.bfloat16),
            span_slice[..., FEATURE_WIDTH:],
            preferred_element_type=jnp.float32,
        )
        return (dec_numer, dec_denom + jnp.sum(weight, axis=-1))

    first_numer = jnp.zeros((DEC, heads_here, HDIM), jnp.float32)
    first_denom = jnp.zeros((DEC, heads_here), jnp.float32)
    decode_blocks = (jnp.max(counts) + block - 1) // block
    dec_numer, dec_denom = lax.fori_loop(0, decode_blocks, decode_step, (first_numer, first_denom))
    taylor_score = (
        jnp.sum(
            decode_queries.astype(jnp.float32) * key_rows[SPAN_TOKENS:].astype(jnp.float32), axis=-1
        )
        * score_scale
    )
    weight = taylor(taylor_score) * live[SPAN_TOKENS:, None]
    dec_numer = dec_numer + weight.astype(jnp.bfloat16).astype(jnp.float32)[..., None] * values[
        SPAN_TOKENS:
    ].astype(jnp.float32)
    dec_denom = dec_denom + weight
    numer_all = jnp.concatenate([jnp.transpose(numer, (1, 0, 2)), dec_numer], axis=0)
    denom_all = jnp.concatenate([jnp.transpose(denom, (1, 0)), dec_denom], axis=0)
    result = live[:, None, None] * numer_all / (denom_all + 1.0 - live[:, None])[..., None]
    return result.astype(jnp.bfloat16).reshape(rows, heads_here * HDIM)


def plain_shards(hidden, norm_gain, qkv_weight, out_weight, cache, cached, token_mask):
    full, gain = (
        lax.all_gather(hidden, "col", axis=1, tiled=True),
        lax.all_gather(norm_gain, "col", axis=0, tiled=True),
    )
    wide = full.astype(jnp.float32)
    normed = (
        wide
        * lax.rsqrt(jnp.mean(wide * wide, axis=-1, keepdims=True) + 1e-06)
        * gain.astype(jnp.float32)
    )
    normed = normed.astype(jnp.bfloat16)
    projected = jnp.dot(
        normed,
        lax.all_gather(qkv_weight, "row", axis=0, tiled=True),
        preferred_element_type=jnp.float32,
    ).astype(jnp.bfloat16)
    attended = attend(projected, cache, cached, token_mask)
    terms = jnp.dot(
        attended,
        lax.all_gather(out_weight, "row", axis=1, tiled=True),
        preferred_element_type=jnp.float32,
    )
    mixed = lax.psum_scatter(terms, "col", scatter_dimension=1, tiled=True).astype(jnp.bfloat16)
    return mixed


def solution(mesh):
    in_specs = (
        P("row", "col"),
        P("col"),
        P("row", "col"),
        P("col", "row"),
        P("row", None, "col"),
        P("row"),
        P("row"),
    )
    out_specs = P("row", "col")
    body = shards if (mesh.shape["row"], mesh.shape["col"]) == (8, 4) else plain_shards
    return jax.shard_map(body, mesh=mesh, in_specs=in_specs, out_specs=out_specs, check_vma=False)
```

```python
import jax
import jax.numpy as jnp
from jax import lax
from jax.experimental import pallas as pl
from jax.experimental.pallas import tpu as pltpu
from jax.sharding import PartitionSpec as P

FEATURE_WIDTH = 16
HDIM = 112
SPAN_TOKENS = 512
DEC = 4
LANES = FEATURE_WIDTH + HDIM
F32 = jnp.float32
BF16 = jnp.bfloat16
HALF = SPAN_TOKENS // 2
VMEM = pl.BlockSpec(memory_space=pltpu.VMEM)
SMEM = pl.BlockSpec(memory_space=pltpu.SMEM)
HBM = pl.BlockSpec(memory_space=pltpu.MemorySpace.HBM)
TAIL = 3 * HALF
BODY = TAIL + HALF // 2
EXTRA = 32
QROWS = 224
OROWS = 448
WROWS = 4 * QROWS + 2 * OROWS
COST_X = 5_000_000_000
COST_SQ = 1_000_000_000
COST_CA = 100_000_000
COST_CB = 1_000_000_000
COST_F = 2_000_000_000
COST_D = 1_000_000


def gray(place):
    return place ^ (place >> 1)


def call(body, outs, in_specs, scratch=(), flops=0, nbytes=0, name=None, mib=8):
    return pl.pallas_call(
        body,
        out_shape=outs,
        in_specs=in_specs,
        out_specs=jax.tree.map(lambda _: VMEM, outs),
        scratch_shapes=scratch,
        cost_estimate=pl.CostEstimate(flops=flops, bytes_accessed=nbytes, transcendentals=0),
        compiler_params=pltpu.CompilerParams(vmem_limit_bytes=mib * 1024 * 1024),
        name=name,
    )


def shaped(shape, dtype=BF16):
    return jax.ShapeDtypeStruct(shape, dtype)


def dot(a, b):
    return jnp.dot(a, b, preferred_element_type=F32)


def dot_nt(a, b):
    return lax.dot_general(a, b, (((1,), (1,)), ((), ())), preferred_element_type=F32)


def lane(shape):
    return lax.broadcasted_iota(jnp.int32, shape, len(shape) - 1)


def row(shape):
    return lax.broadcasted_iota(jnp.int32, shape, 0)


def pack(hidden, gains, qkv, outs, a_ref, b_ref, w_ref, h_ref, g_ref, q_ref, o_ref, sems):
    pairs = ((hidden, h_ref), (gains, g_ref), (qkv, q_ref), (outs, o_ref))
    copies = [pltpu.make_async_copy(*pair, sems.at[n]) for n, pair in enumerate(pairs)]
    for copy in copies:
        copy.start()
    copies[0].wait()
    copies[1].wait()
    for ref, base in ((a_ref, 0), (b_ref, HALF)):
        for t in range(3):
            ref[t * HALF : (t + 1) * HALF, :] = h_ref[base : base + HALF, t * 128 : (t + 1) * 128]
        low = h_ref[base : base + HALF // 2, 384:448]
        high = h_ref[base + HALF // 2 : base + HALF, 384:448]
        ref[TAIL:BODY, :] = jnp.concatenate([low, high], axis=1)
        ref[BODY:, :] = jnp.zeros((EXTRA, 128), BF16)
    gain = g_ref[...].reshape(1, 448)
    for t in range(3):
        a_ref[BODY + 8 * t : BODY + 8 * t + 1, :] = gain[:, t * 128 : (t + 1) * 128]
        b_ref[BODY + 8 * t : BODY + 8 * t + DEC, :] = h_ref[SPAN_TOKENS:, t * 128 : (t + 1) * 128]
    last = gain[:, 384:448]
    a_ref[BODY + 24 : BODY + 25, :] = jnp.concatenate([last, last], axis=1)
    b_ref[BODY + 24 : BODY + 24 + DEC, 0:64] = h_ref[SPAN_TOKENS:, 384:448]
    copies[2].wait()
    copies[3].wait()
    width = FEATURE_WIDTH + LANES
    for h in range(4):
        w_ref[h * QROWS : (h + 1) * QROWS, :] = q_ref[:, h * width + FEATURE_WIDTH : (h + 1) * width]
    at = 4 * QROWS
    w_ref[at : at + OROWS, :] = o_ref[:, 0:128]
    for side in range(2):
        pieces = [o_ref[side * QROWS : (side + 1) * QROWS, 128:224]]
        for h in (2 * side, 2 * side + 1):
            pieces.append(q_ref[:, h * width : h * width + FEATURE_WIDTH])
        rows = at + OROWS + side * QROWS
        w_ref[rows : rows + QROWS, :] = jnp.concatenate(pieces, axis=1)


def place_weights(*refs):
    blocks, (w_ref, o_ref) = refs[:8], refs[8:]
    me = lax.axis_index("row")
    at, late = 4 * QROWS, 4 * QROWS + OROWS

    def project_rows(block):
        queries = [block[late + s * QROWS : late + (s + 1) * QROWS, 96:128] for s in range(2)]
        queries.append(jnp.zeros((QROWS, 64), BF16))
        heads = [block[h * QROWS : (h + 1) * QROWS, :] for h in range(4)]
        return heads + [jnp.concatenate(queries, axis=1)]

    for core in range(2):

        @pl.when(me & 1 == core)
        def _():
            for k in range(4):
                j = (me >> 1) ^ k
                low, high = blocks[2 * k + core], blocks[2 * k + 1 - core]
                for t, tile in enumerate(project_rows(low)):
                    w_ref[j, 0:QROWS, t * 128 : (t + 1) * 128] = tile
                for t, tile in enumerate(project_rows(high)):
                    w_ref[j, QROWS : 2 * QROWS, t * 128 : (t + 1) * 128] = tile
                    w_ref[j, 448:512, t * 128 : (t + 1) * 128] = tile[160:QROWS, :]
                full = jnp.concatenate(
                    [low[at:late, :], low[late:, 0:96], high[at:late, :], high[late:, 0:96]], axis=1
                )
                full = jnp.concatenate([full, full[:, 384:448]], axis=1)
                for h in range(4):
                    o_ref[j, h * LANES : h * LANES + FEATURE_WIDTH, :] = jnp.zeros((FEATURE_WIDTH, 512), BF16)
                    o_ref[j, h * LANES + FEATURE_WIDTH : (h + 1) * LANES, :] = full[h * HDIM : (h + 1) * HDIM, :]


def as_keys(kv):
    return jnp.where(lane(kv.shape) % LANES == FEATURE_WIDTH, 1.0, kv).astype(BF16)


def as_values(kv, keep):
    ones = jnp.where(lane(kv.shape) % LANES < FEATURE_WIDTH, 1.0, kv)
    return jnp.where(keep, ones, 0.0).astype(BF16)


def prepare_cache(cache, len_ref, k_ref, v_ref, slab, sem):
    copy = pltpu.make_async_copy(cache.at[0], slab, sem)
    copy.start()
    copy.wait()
    kv = slab[...].astype(F32)
    k_ref[...] = as_keys(kv)
    v_ref[...] = as_values(kv, row(kv.shape) < len_ref[0])


def tiles_of(ref, rows):
    middle = lane((HALF // 2, 128)) < 64
    tail = ref[TAIL:BODY, :].astype(F32)
    tail = jnp.concatenate([jnp.where(middle, tail, 0.0), jnp.where(middle, 0.0, tail)], axis=0)
    tiles = [ref[t * HALF : (t + 1) * HALF, :].astype(F32) for t in range(3)] + [tail]
    if rows > HALF:
        late = [ref[BODY + 8 * t : BODY + 8 * t + 8, :].astype(F32) for t in range(4)]
        zeros = jnp.zeros((8, 128), F32)
        tiles = [jnp.concatenate(parts + (zeros,), axis=0) for parts in zip(tiles, late)]
    return tiles


def squares(tiles):
    total = tiles[0] * tiles[0]
    for tile in tiles[1:]:
        total = total + tile * tile
    return total


def square_b(ref, out):
    out[...] = squares(tiles_of(ref, HALF + 16))


def norm(blocks, gain_ref, sums, out_ref, rows):
    pieces = [tiles_of(ref, rows) for ref in blocks]
    total = None
    for k, tiles in enumerate(pieces):
        part = sums[k][...] if k in sums else squares(tiles)
        total = part if total is None else total + part
    mean = jnp.sum(total, axis=1, keepdims=True) * (1.0 / 1792.0)
    scale = jnp.broadcast_to(lax.rsqrt(mean + 1e-06), (rows, 128))
    for k, tiles in enumerate(pieces):
        for t, tile in enumerate(tiles):
            gain = gain_ref[k][BODY + 8 * t : BODY + 8 * t + 1, :].astype(F32)
            out_ref[:, k * 512 + t * 128 : k * 512 + (t + 1) * 128] = (tile * scale * gain).astype(BF16)


def norm_a(a0, a1, a2, a3, out):
    norm((a0, a1, a2, a3), (a0, a1, a2, a3), {}, out, HALF)


def norm_b(b0, b1, b2, b3, s1, s2, a0, a1, a2, a3, out):
    norm((b0, b1, b2, b3), (a0, a1, a2, a3), {1: s1, 2: s2}, out, HALF + 16)


def project(normed, w_ref):
    place = gray(lax.axis_index("col"))
    total = None
    for k in range(4):
        term = dot(normed[:, k * 512 : (k + 1) * 512], w_ref[gray((place + 4 - k) & 3)])
        total = term if total is None else total + term
    total = total.astype(BF16).astype(F32)
    return total[:, 0:512], total[:, 512:640]


def query_of(queries, h):
    q = pltpu.roll(queries, (128 - FEATURE_WIDTH * h) % 128, 1) if h else queries
    at = lane(q.shape)
    return jnp.where(at < FEATURE_WIDTH, q * FEATURE_WIDTH**-0.5, 0.0), at == FEATURE_WIDTH


def weigh(scores, keep=None):
    weight = scores * scores + 1.0
    if keep is not None:
        weight = jnp.where(keep, weight, 0.0)
    return weight.astype(BF16)


def divide(total, mask):
    below = jnp.broadcast_to(total[:, 0:1], total.shape) + 2.0 * (1.0 - mask)
    return mask * total / below


def emit(att, o_ref, first_ref, rest):
    place = gray(lax.axis_index("col"))
    for s in range(4):
        part = dot(att, o_ref[gray((place + 3 - s) & 3)])
        out = first_ref if s == 0 else rest[s - 1]
        for t in range(3):
            out[t * HALF : (t + 1) * HALF, :] = part[:HALF, t * 128 : (t + 1) * 128].astype(out.dtype)
        last = part[:, 384:512]
        middle = lane((HALF // 2, 128)) < 64
        out[TAIL:BODY, :] = jnp.where(middle, last[: HALF // 2], last[HALF // 2 : HALF]).astype(out.dtype)


def chunk_a(normed, w_ref, o_ref, ck_ref, cv_ref, m_ref, first, r1, r2, r3, ka_ref, va_ref):
    kv, queries = project(normed, w_ref)
    mask = m_ref[0:HALF, :]
    ka_ref[...] = as_keys(kv)
    va_ref[...] = as_values(kv, jnp.concatenate([mask] * 4, axis=1) > 0.0)
    causal = lane((HALF, HALF)) <= row((HALF, HALF))
    outs = []
    for h in range(4):
        at = slice(h * LANES, (h + 1) * LANES)
        q, one = query_of(queries, h)
        q = jnp.where(one, 1.0, q).astype(BF16)
        total = dot(weigh(dot_nt(q, ka_ref[:, at]), causal), va_ref[:, at])
        for b in range(2):
            keys = slice(b * 512, (b + 1) * 512)
            total += dot(weigh(dot_nt(q, ck_ref[keys, at])), cv_ref[keys, at])
        outs.append(divide(total, mask).astype(BF16))
    emit(jnp.concatenate(outs, axis=1), o_ref, first, (r1, r2, r3))


def chunk_b(
    normed, w_ref, o_ref, ck_ref, cv_ref, m_ref, ka_ref, va_ref, first, r1, r2, r3, late_ref, kb, vb
):
    kv, queries = project(normed, w_ref)
    late_ref[:, 0:512] = kv[HALF:]
    late_ref[:, 512:640] = queries[HALF:]
    kv, queries = kv[:HALF], queries[:HALF]
    mask = m_ref[HALF : 2 * HALF, :]
    kb[...] = as_keys(kv)
    vb[...] = as_values(kv, jnp.concatenate([mask] * 4, axis=1) > 0.0)
    causal = lane((HALF, HALF)) <= row((HALF, HALF))
    outs = []
    for h in range(4):
        at = slice(h * LANES, (h + 1) * LANES)
        q, one = query_of(queries, h)
        q = jnp.where(one, 1.0, q).astype(BF16)
        total = dot(weigh(dot_nt(q, kb[:, at]), causal), vb[:, at])
        total += dot(weigh(dot_nt(q, ka_ref[:, at])), va_ref[:, at])
        for b in range(2):
            keys = slice(b * 512, (b + 1) * 512)
            total += dot(weigh(dot_nt(q, ck_ref[keys, at])), cv_ref[keys, at])
        outs.append(divide(total, mask).astype(BF16))
    emit(jnp.concatenate(outs, axis=1), o_ref, first, (r1, r2, r3))


def decode(late_ref, o_ref, m_ref, len_ref, cache, own_ref, s1, s2, s3, slab, sems):
    copies = [pltpu.make_async_copy(cache.at[d + 1], slab.at[d], sems.at[d]) for d in range(DEC)]
    for copy in copies:
        copy.start()
    fresh = late_ref[:, 0:512]
    late = jnp.concatenate([query_of(late_ref[:, 512:640], h)[0] for h in range(4)], axis=1)
    own = row((16, 512)) == lane((16, 512)) // LANES
    position = lane((16, 1024))
    decoded = jnp.zeros((16, 512), F32)
    for d in range(DEC):
        copies[d].wait()
        q = jnp.where(own, jnp.broadcast_to(late[d : d + 1], (16, 512)), 0.0)
        new = jnp.broadcast_to(fresh[d : d + 1], (16, 512))
        live = m_ref[2 * HALF + d : 2 * HALF + d + 1, 0:1]
        score = dot_nt(q.astype(BF16), slab[d]) + 1.0
        weight = jnp.where(position < len_ref[d + 1], score * score + 1.0, 0.0)
        self_score = jnp.sum(q * new, axis=1, keepdims=True) + 1.0
        self_weight = (self_score * self_score + 1.0) * live
        total = dot(weight.astype(BF16), slab[d]) + self_weight.astype(BF16).astype(F32) * new
        below = jnp.sum(weight, axis=1, keepdims=True) + self_weight + 2.0 * (1.0 - live)
        value = jnp.sum(jnp.where(own, live * total / below, 0.0), axis=0, keepdims=True)
        decoded = jnp.where(row((16, 512)) == d, jnp.broadcast_to(value, (16, 512)), decoded)
    me = lax.axis_index("col")
    for k, out in enumerate((own_ref, s1, s2, s3)):
        out[...] = dot(decoded.astype(BF16), o_ref[(me + k) & 3])[0:8]


def unpack_sum(recv, part, out, base):
    for t in range(3):
        at = slice(t * HALF, (t + 1) * HALF)
        out[base : base + HALF, t * 128 : (t + 1) * 128] = (recv[at, :].astype(F32) + part[at, :]).astype(BF16)
    tail = recv[TAIL:BODY, :].astype(F32) + part[TAIL:BODY, :]
    out[base : base + HALF // 2, 384:448] = tail[:, 0:64].astype(BF16)
    out[base + HALF // 2 : base + HALF, 384:448] = tail[:, 64:128].astype(BF16)


def finish_a(recv, part, p0, p1, p2, p3, out, late):
    unpack_sum(recv, part, out, 0)
    late[...] = ((p0[...] + p1[...]) + (p2[...] + p3[...])).astype(BF16)


def finish_b(done, late, recv, part, out):
    out[:HALF, :] = done[...]
    unpack_sum(recv, part, out, HALF)
    out[SPAN_TOKENS:, :] = late[0:DEC, 0:448]


def in_hbm(x):
    return pltpu.with_memory_space_constraint(x, pltpu.MemorySpace.HBM)


def after(value, *others):
    return lax.optimization_barrier((value, *others))[0]


def shards(hidden, norm_gain, qkv_weight, out_weight, cache, cached, token_mask):
    ring = [(gray(p), gray((p + 1) % 4)) for p in range(4)]

    def onward(x):
        return lax.ppermute(x, "col", ring)

    def across(x, k):
        return lax.ppermute(x, "row", [(i, i ^ k) for i in range(8)])

    a, b, own = call(
        pack,
        (shaped((BODY + EXTRA, 128)), shaped((BODY + EXTRA, 128)), shaped((WROWS, 128))),
        [HBM] * 4,
        scratch=[pltpu.VMEM(x.shape, BF16) for x in (hidden, norm_gain, qkv_weight, out_weight)]
        + [pltpu.SemaphoreType.DMA((4,))],
        nbytes=300_000,
        name="pack",
    )(*(in_hbm(x) for x in (hidden, norm_gain, qkv_weight, out_weight)))
    plane = [own] + [across(own, k) for k in (2, 4, 6)]

    def sums(x, name):
        return call(square_b, shaped((HALF + 16, 128), F32), [VMEM], flops=COST_SQ, nbytes=300_000, name=name)(x)

    a1, b1 = onward(a), onward(b)
    a2, b2 = onward(a1), onward(b1)
    s1, s2 = sums(b1, "square_b1"), sums(b2, "square_b2")
    a3 = after(onward(after(a2, s1)), s2, *plane[1:])
    a, b = [a, a1, a2, a3], [b, b1, b2, onward(b2)]
    blocks = [own, across(after(own, s2), 1)]
    for block in plane[1:]:
        blocks += [block, across(block, 1)]
    w, o = call(
        place_weights,
        (shaped((4, 512, 640)), shaped((4, 512, 512))),
        [VMEM] * 8,
        nbytes=300_000,
        name="place_weights",
    )(*blocks)
    na = call(norm_a, shaped((HALF, 2048)), [VMEM] * 4, flops=COST_X, nbytes=300_000, name="norm_a")(*a)
    nb = call(norm_b, shaped((HALF + 16, 2048)), [VMEM] * 10, nbytes=300_000, name="norm_b")(
        *b, s1, s2, *a
    )
    ck, cv = call(
        prepare_cache,
        (shaped((1024, 512)), shaped((1024, 512))),
        [HBM, SMEM],
        scratch=[pltpu.VMEM((1024, 512), BF16), pltpu.SemaphoreType.DMA],
        nbytes=300_000,
        name="prepare_cache",
        mib=12,
    )(in_hbm(cache), cached)
    mask = jnp.broadcast_to(token_mask.astype(F32)[:, None], (token_mask.shape[0], 128))
    body = shaped((BODY, 128), F32)
    first, *rest_a, ka, va = call(
        chunk_a,
        (shaped((BODY, 128)), body, body, body, shaped((HALF, 512)), shaped((HALF, 512))),
        [VMEM] * 6,
        flops=COST_CA,
        nbytes=300_000,
        name="chunk_a",
        mib=20,
    )(na, w, o, ck, cv, mask)
    send_a = onward(first)
    first, *rest_b, late = call(
        chunk_b,
        (shaped((BODY, 128)), body, body, body, shaped((16, 640), F32)),
        [VMEM] * 8,
        scratch=[pltpu.VMEM((HALF, 512), BF16), pltpu.VMEM((HALF, 512), BF16)],
        flops=COST_CB,
        nbytes=300_000,
        name="chunk_b",
        mib=20,
    )(nb, w, o, ck, cv, mask, ka, va)
    send_b = onward(first)
    few = shaped((8, 512), F32)
    parts = call(
        decode,
        (few, few, few, few),
        [VMEM] * 3 + [SMEM, HBM],
        scratch=[pltpu.VMEM((DEC, 1024, 512), BF16), pltpu.SemaphoreType.DMA((DEC,))],
        flops=COST_D,
        nbytes=300_000,
        name="decode",
        mib=12,
    )(late, o, mask, cached, in_hbm(cache))
    send_a = onward((send_a.astype(F32) + rest_a[0]).astype(BF16))
    send_b = onward((after(send_b, parts[0]).astype(F32) + rest_b[0]).astype(BF16))
    send_a = onward((send_a.astype(F32) + rest_a[1]).astype(BF16))
    send_b = onward((send_b.astype(F32) + rest_b[1]).astype(BF16))
    parts = parts[:1] + tuple(
        lax.ppermute(parts[k], "col", [(i, (i + k) % 4) for i in range(4)]) for k in (1, 2, 3)
    )
    done, late = call(
        finish_a,
        (shaped((HALF, hidden.shape[1])), shaped((8, 512))),
        [VMEM] * 6,
        flops=COST_F,
        nbytes=300_000,
        name="finish_a",
    )(send_a, rest_a[2], *parts)
    return call(finish_b, shaped(hidden.shape), [VMEM] * 4, nbytes=300_000, name="finish_b")(
        done, late, send_b, rest_b[2]
    )


def taylor(taylor_score):
    return 1.0 + taylor_score + 0.5 * taylor_score * taylor_score


def attend(projected, cache, cached, token_mask):
    rows = projected.shape[0]
    width = 2 * FEATURE_WIDTH + HDIM
    lanes = FEATURE_WIDTH + HDIM
    heads_here = projected.shape[1] // width
    parts = projected.reshape(rows, heads_here, width)
    query_rows = parts[:, :, :FEATURE_WIDTH]
    key_rows = parts[:, :, FEATURE_WIDTH : 2 * FEATURE_WIDTH]
    values = parts[:, :, 2 * FEATURE_WIDTH :]
    store = cache.reshape(cache.shape[0], cache.shape[1], heads_here, lanes)
    capacity = cache.shape[1]
    block = min(512, capacity)
    score_scale = FEATURE_WIDTH ** (-0.5)
    live = token_mask.astype(jnp.float32)
    prefill_query_rows = query_rows[:SPAN_TOKENS]
    prior_tokens = store[0]
    offset = cached[0]

    def span_step(index, carry):
        numer, denom = carry
        span_slice = lax.dynamic_slice_in_dim(prior_tokens, index * block, block, 0)
        position = index * block + lax.iota(jnp.int32, block)
        taylor_score = (
            jnp.einsum(
                "sue,pue->usp",
                prefill_query_rows,
                span_slice[:, :, :FEATURE_WIDTH],
                preferred_element_type=jnp.float32,
            )
            * score_scale
        )
        weight = taylor(taylor_score) * (position < offset).astype(jnp.float32)[None, None, :]
        numer = numer + jnp.einsum(
            "hqk,khd->hqd",
            weight.astype(jnp.bfloat16),
            span_slice[:, :, FEATURE_WIDTH:],
            preferred_element_type=jnp.float32,
        )
        return (numer, denom + jnp.sum(weight, axis=-1))

    start_numer = jnp.zeros((heads_here, SPAN_TOKENS, HDIM), jnp.float32)
    start_denom = jnp.zeros((heads_here, SPAN_TOKENS), jnp.float32)
    span_blocks = (offset + block - 1) // block
    numer, denom = lax.fori_loop(0, span_blocks, span_step, (start_numer, start_denom))
    taylor_score = (
        jnp.einsum(
            "sue,pue->usp",
            prefill_query_rows,
            key_rows[:SPAN_TOKENS],
            preferred_element_type=jnp.float32,
        )
        * score_scale
    )
    order = lax.iota(jnp.int32, SPAN_TOKENS)
    allowed = (order[None, :] <= order[:, None]).astype(jnp.float32) * live[:SPAN_TOKENS][None, :]
    weight = taylor(taylor_score) * allowed[None]
    numer = numer + jnp.einsum(
        "hqk,khd->hqd",
        weight.astype(jnp.bfloat16),
        values[:SPAN_TOKENS],
        preferred_element_type=jnp.float32,
    )
    denom = denom + jnp.sum(weight, axis=-1)
    decode_queries = query_rows[SPAN_TOKENS:]
    past = store[1:]
    counts = cached[1:]

    def decode_step(index, carry):
        dec_numer, dec_denom = carry
        span_slice = lax.dynamic_slice_in_dim(past, index * block, block, 1)
        position = index * block + lax.iota(jnp.int32, block)
        taylor_score = (
            jnp.einsum(
                "rhf,rkhf->rhk",
                decode_queries,
                span_slice[..., :FEATURE_WIDTH],
                preferred_element_type=jnp.float32,
            )
            * score_scale
        )
        seen = (position[None, :] < counts[:, None]).astype(jnp.float32)
        weight = taylor(taylor_score) * seen[:, None, :]
        dec_numer = dec_numer + jnp.einsum(
            "rhk,rkhd->rhd",
            weight.astype(jnp.bfloat16),
            span_slice[..., FEATURE_WIDTH:],
            preferred_element_type=jnp.float32,
        )
        return (dec_numer, dec_denom + jnp.sum(weight, axis=-1))

    first_numer = jnp.zeros((DEC, heads_here, HDIM), jnp.float32)
    first_denom = jnp.zeros((DEC, heads_here), jnp.float32)
    decode_blocks = (jnp.max(counts) + block - 1) // block
    dec_numer, dec_denom = lax.fori_loop(0, decode_blocks, decode_step, (first_numer, first_denom))
    taylor_score = (
        jnp.sum(
            decode_queries.astype(jnp.float32) * key_rows[SPAN_TOKENS:].astype(jnp.float32), axis=-1
        )
        * score_scale
    )
    weight = taylor(taylor_score) * live[SPAN_TOKENS:, None]
    dec_numer = dec_numer + weight.astype(jnp.bfloat16).astype(jnp.float32)[..., None] * values[
        SPAN_TOKENS:
    ].astype(jnp.float32)
    dec_denom = dec_denom + weight
    numer_all = jnp.concatenate([jnp.transpose(numer, (1, 0, 2)), dec_numer], axis=0)
    denom_all = jnp.concatenate([jnp.transpose(denom, (1, 0)), dec_denom], axis=0)
    result = live[:, None, None] * numer_all / (denom_all + 1.0 - live[:, None])[..., None]
    return result.astype(jnp.bfloat16).reshape(rows, heads_here * HDIM)


def plain_shards(hidden, norm_gain, qkv_weight, out_weight, cache, cached, token_mask):
    full, gain = (
        lax.all_gather(hidden, "col", axis=1, tiled=True),
        lax.all_gather(norm_gain, "col", axis=0, tiled=True),
    )
    wide = full.astype(jnp.float32)
    normed = (
        wide
        * lax.rsqrt(jnp.mean(wide * wide, axis=-1, keepdims=True) + 1e-06)
        * gain.astype(jnp.float32)
    )
    normed = normed.astype(jnp.bfloat16)
    projected = jnp.dot(
        normed,
        lax.all_gather(qkv_weight, "row", axis=0, tiled=True),
        preferred_element_type=jnp.float32,
    ).astype(jnp.bfloat16)
    attended = attend(projected, cache, cached, token_mask)
    terms = jnp.dot(
        attended,
        lax.all_gather(out_weight, "row", axis=1, tiled=True),
        preferred_element_type=jnp.float32,
    )
    mixed = lax.psum_scatter(terms, "col", scatter_dimension=1, tiled=True).astype(jnp.bfloat16)
    return mixed


def solution(mesh):
    in_specs = (
        P("row", "col"),
        P("col"),
        P("row", "col"),
        P("col", "row"),
        P("row", None, "col"),
        P("row"),
        P("row"),
    )
    out_specs = P("row", "col")
    body = shards if (mesh.shape["row"], mesh.shape["col"]) == (8, 4) else plain_shards
    return jax.shard_map(body, mesh=mesh, in_specs=in_specs, out_specs=out_specs, check_vma=False)
```

```python
import jax
import jax.numpy as jnp
from jax import lax
from jax.experimental import pallas as pl
from jax.experimental.pallas import tpu as pltpu
from jax.sharding import PartitionSpec as P

FEATURE_WIDTH = 16
HDIM = 112
SPAN_TOKENS = 512
DEC = 4
LANES = FEATURE_WIDTH + HDIM
F32 = jnp.float32
BF16 = jnp.bfloat16
HALF = SPAN_TOKENS // 2
VMEM = pl.BlockSpec(memory_space=pltpu.VMEM)
SMEM = pl.BlockSpec(memory_space=pltpu.SMEM)
HBM = pl.BlockSpec(memory_space=pltpu.MemorySpace.HBM)
TAIL = 3 * HALF
BODY = TAIL + HALF // 2
EXTRA = 16
QROWS = 224
OROWS = 448
WROWS = 4 * QROWS + 2 * OROWS
COST_X = 5_000_000_000
COST_SQ = 1_000_000_000
COST_CA = 100_000_000
COST_CB = 1_000_000_000
COST_F = 1_000_000
COST_G = 10_000_000
COST_D = 1_000_000
COST_E = 1_000_000


def gray(place):
    return place ^ (place >> 1)


def call(body, outs, in_specs, scratch=(), flops=0, nbytes=0, name=None, mib=8):
    return pl.pallas_call(
        body,
        out_shape=outs,
        in_specs=in_specs,
        out_specs=jax.tree.map(lambda _: VMEM, outs),
        scratch_shapes=scratch,
        cost_estimate=pl.CostEstimate(flops=flops, bytes_accessed=nbytes, transcendentals=0),
        compiler_params=pltpu.CompilerParams(vmem_limit_bytes=mib * 1024 * 1024),
        name=name,
    )


def shaped(shape, dtype=BF16):
    return jax.ShapeDtypeStruct(shape, dtype)


def dot(a, b):
    return jnp.dot(a, b, preferred_element_type=F32)


def dot_nt(a, b):
    return lax.dot_general(a, b, (((1,), (1,)), ((), ())), preferred_element_type=F32)


def lane(shape):
    return lax.broadcasted_iota(jnp.int32, shape, len(shape) - 1)


def row(shape):
    return lax.broadcasted_iota(jnp.int32, shape, 0)


def pack(hidden, gains, qkv, outs, a_ref, b_ref, w_ref, h_ref, g_ref, q_ref, o_ref, sems):
    pairs = ((hidden, h_ref), (gains, g_ref), (qkv, q_ref), (outs, o_ref))
    copies = [pltpu.make_async_copy(*pair, sems.at[n]) for n, pair in enumerate(pairs)]
    for copy in copies:
        copy.start()
    copies[0].wait()
    copies[1].wait()
    for ref, base in ((a_ref, 0), (b_ref, HALF)):
        for t in range(3):
            ref[t * HALF : (t + 1) * HALF, :] = h_ref[base : base + HALF, t * 128 : (t + 1) * 128]
        low = h_ref[base : base + HALF // 2, 384:448]
        high = h_ref[base + HALF // 2 : base + HALF, 384:448]
        ref[TAIL:BODY, :] = jnp.concatenate([low, high], axis=1)
        ref[BODY:, :] = jnp.zeros((EXTRA, 128), BF16)
    gain = g_ref[...].reshape(1, 448)
    for t in range(3):
        a_ref[BODY + t : BODY + t + 1, :] = gain[:, t * 128 : (t + 1) * 128]
        b_ref[BODY + DEC * t : BODY + DEC * (t + 1), :] = h_ref[SPAN_TOKENS:, t * 128 : (t + 1) * 128]
    last = gain[:, 384:448]
    a_ref[BODY + 3 : BODY + 4, :] = jnp.concatenate([last, last], axis=1)
    b_ref[BODY + 3 * DEC :, 0:64] = h_ref[SPAN_TOKENS:, 384:448]
    copies[2].wait()
    copies[3].wait()
    width = FEATURE_WIDTH + LANES
    for h in range(4):
        w_ref[h * QROWS : (h + 1) * QROWS, :] = q_ref[:, h * width + FEATURE_WIDTH : (h + 1) * width]
    at = 4 * QROWS
    w_ref[at : at + OROWS, :] = o_ref[:, 0:128]
    for side in range(2):
        pieces = [o_ref[side * QROWS : (side + 1) * QROWS, 128:224]]
        for h in (2 * side, 2 * side + 1):
            pieces.append(q_ref[:, h * width : h * width + FEATURE_WIDTH])
        rows = at + OROWS + side * QROWS
        w_ref[rows : rows + QROWS, :] = jnp.concatenate(pieces, axis=1)


def place_weights(*refs):
    blocks, (w_ref, o_ref) = refs[:8], refs[8:]
    me = lax.axis_index("row")
    at, late = 4 * QROWS, 4 * QROWS + OROWS

    def project_rows(block):
        queries = [block[late + s * QROWS : late + (s + 1) * QROWS, 96:128] for s in range(2)]
        queries.append(jnp.zeros((QROWS, 64), BF16))
        heads = [block[h * QROWS : (h + 1) * QROWS, :] for h in range(4)]
        return heads + [jnp.concatenate(queries, axis=1)]

    for core in range(2):

        @pl.when(me & 1 == core)
        def _():
            for k in range(4):
                j = (me >> 1) ^ k
                low, high = blocks[2 * k + core], blocks[2 * k + 1 - core]
                for t, tile in enumerate(project_rows(low)):
                    w_ref[j, 0:QROWS, t * 128 : (t + 1) * 128] = tile
                for t, tile in enumerate(project_rows(high)):
                    w_ref[j, QROWS : 2 * QROWS, t * 128 : (t + 1) * 128] = tile
                    w_ref[j, 448:512, t * 128 : (t + 1) * 128] = tile[160:QROWS, :]
                full = jnp.concatenate(
                    [low[at:late, :], low[late:, 0:96], high[at:late, :], high[late:, 0:96]], axis=1
                )
                full = jnp.concatenate([full, full[:, 384:448]], axis=1)
                for h in range(4):
                    o_ref[j, h * LANES : h * LANES + FEATURE_WIDTH, :] = jnp.zeros((FEATURE_WIDTH, 512), BF16)
                    o_ref[j, h * LANES + FEATURE_WIDTH : (h + 1) * LANES, :] = full[h * HDIM : (h + 1) * HDIM, :]


def as_keys(kv):
    return jnp.where(lane(kv.shape) % LANES == FEATURE_WIDTH, 1.0, kv).astype(BF16)


def as_values(kv, keep):
    ones = jnp.where(lane(kv.shape) % LANES < FEATURE_WIDTH, 1.0, kv)
    return jnp.where(keep, ones, 0.0).astype(BF16)


def prepare_cache(cache, len_ref, k_ref, v_ref, slab, sem):
    copy = pltpu.make_async_copy(cache.at[0], slab, sem)
    copy.start()
    copy.wait()
    kv = slab[...].astype(F32)
    k_ref[...] = as_keys(kv)
    v_ref[...] = as_values(kv, row(kv.shape) < len_ref[0])


def tiles_of(ref, rows):
    middle = lane((HALF // 2, 128)) < 64
    tail = ref[TAIL:BODY, :].astype(F32)
    tail = jnp.concatenate([jnp.where(middle, tail, 0.0), jnp.where(middle, 0.0, tail)], axis=0)
    tiles = [ref[t * HALF : (t + 1) * HALF, :].astype(F32) for t in range(3)] + [tail]
    if rows > HALF:
        extra = ref[BODY:, :].astype(F32)
        late = [extra[DEC * t : DEC * (t + 1), :] for t in range(4)]
        zeros = jnp.zeros((16 - DEC, 128), F32)
        tiles = [jnp.concatenate(parts + (zeros,), axis=0) for parts in zip(tiles, late)]
    return tiles


def squares(tiles):
    total = tiles[0] * tiles[0]
    for tile in tiles[1:]:
        total = total + tile * tile
    return total


def square_b(ref, out):
    out[...] = squares(tiles_of(ref, HALF + 16))


def norm(blocks, gain_ref, sums, out_ref, rows):
    pieces = [tiles_of(ref, rows) for ref in blocks]
    total = None
    for k, tiles in enumerate(pieces):
        part = sums[k][...] if k in sums else squares(tiles)
        total = part if total is None else total + part
    mean = jnp.sum(total, axis=1, keepdims=True) * (1.0 / 1792.0)
    scale = jnp.broadcast_to(lax.rsqrt(mean + 1e-06), (rows, 128))
    for k, tiles in enumerate(pieces):
        for t, tile in enumerate(tiles):
            gain = gain_ref[k][BODY + t : BODY + t + 1, :].astype(F32)
            out_ref[:, k * 512 + t * 128 : k * 512 + (t + 1) * 128] = (tile * scale * gain).astype(BF16)


def norm_a(a0, a1, a2, a3, out):
    norm((a0, a1, a2, a3), (a0, a1, a2, a3), {}, out, HALF)


def project(normed, w_ref):
    place = gray(lax.axis_index("col"))
    total = None
    for k in range(4):
        term = dot(normed[:, k * 512 : (k + 1) * 512], w_ref[gray((place + 4 - k) & 3)])
        total = term if total is None else total + term
    total = total.astype(BF16).astype(F32)
    return total[:, 0:512], total[:, 512:640]


def query_of(queries, h):
    q = pltpu.roll(queries, (128 - FEATURE_WIDTH * h) % 128, 1) if h else queries
    at = lane(q.shape)
    return jnp.where(at < FEATURE_WIDTH, q * FEATURE_WIDTH**-0.5, 0.0), at == FEATURE_WIDTH


def weigh(scores, keep=None):
    weight = scores * scores + 1.0
    if keep is not None:
        weight = jnp.where(keep, weight, 0.0)
    return weight.astype(BF16)


def divide(total, mask):
    below = jnp.broadcast_to(total[:, 0:1], total.shape) + 2.0 * (1.0 - mask)
    return mask * total / below


def emit(att, o_ref, outs, start, recv=None):
    place = gray(lax.axis_index("col"))
    middle = lane((HALF // 2, 128)) < 64
    for s, out in enumerate(outs, start):
        part = dot(att, o_ref[gray((place + 3 - s) & 3)])
        tiles = [part[:, t * 128 : (t + 1) * 128] for t in range(3)]
        last = part[:, 384:512]
        tiles.append(jnp.where(middle, last[: HALF // 2], last[HALF // 2 :]))
        for t, tile in enumerate(tiles):
            at = slice(t * HALF, t * HALF + tile.shape[0])
            if recv is not None:
                tile = tile + recv[at, :].astype(F32)
            out[at, :] = tile.astype(out.dtype)


def hop_1(att_ref, o_ref, recv, out):
    emit(att_ref[...], o_ref, (out,), 1, recv)


def hop_2(att_ref, o_ref, recv, out):
    emit(att_ref[...], o_ref, (out,), 2, recv)


def hop_3(att_ref, o_ref, out):
    emit(att_ref[...], o_ref, (out,), 3)


def chunk_a(normed, w_ref, o_ref, ck_ref, cv_ref, m_ref, first, r1, r2, r3, ka_ref, va_ref):
    kv, queries = project(normed, w_ref)
    mask = m_ref[0:HALF, :]
    ka_ref[...] = as_keys(kv)
    va_ref[...] = as_values(kv, jnp.concatenate([mask] * 4, axis=1) > 0.0)
    causal = lane((HALF, HALF)) <= row((HALF, HALF))
    outs = []
    for h in range(4):
        at = slice(h * LANES, (h + 1) * LANES)
        q, one = query_of(queries, h)
        q = jnp.where(one, 1.0, q).astype(BF16)
        total = dot(weigh(dot_nt(q, ka_ref[:, at]), causal), va_ref[:, at])
        for b in range(2):
            keys = slice(b * 512, (b + 1) * 512)
            total += dot(weigh(dot_nt(q, ck_ref[keys, at])), cv_ref[keys, at])
        outs.append(divide(total, mask).astype(BF16))
    emit(jnp.concatenate(outs, axis=1), o_ref, (first, r1, r2, r3), 0)


def chunk_b(
    b0, b1, b2, b3, s1, s2, a0, a1, a2, a3, w_ref, o_ref, ck_ref, cv_ref, m_ref, ka_ref, va_ref, first, att_ref, late_ref, normed, kb, vb
):
    norm((b0, b1, b2, b3), (a0, a1, a2, a3), {1: s1, 2: s2}, normed, HALF + 16)
    kv, queries = project(normed, w_ref)
    late_ref[:, 0:512] = kv[HALF:]
    late_ref[:, 512:640] = queries[HALF:]
    kv, queries = kv[:HALF], queries[:HALF]
    mask = m_ref[HALF : 2 * HALF, :]
    kb[...] = as_keys(kv)
    vb[...] = as_values(kv, jnp.concatenate([mask] * 4, axis=1) > 0.0)
    causal = lane((HALF, HALF)) <= row((HALF, HALF))
    outs = []
    for h in range(4):
        at = slice(h * LANES, (h + 1) * LANES)
        q, one = query_of(queries, h)
        q = jnp.where(one, 1.0, q).astype(BF16)
        total = dot(weigh(dot_nt(q, kb[:, at]), causal), vb[:, at])
        total += dot(weigh(dot_nt(q, ka_ref[:, at])), va_ref[:, at])
        for b in range(2):
            keys = slice(b * 512, (b + 1) * 512)
            total += dot(weigh(dot_nt(q, ck_ref[keys, at])), cv_ref[keys, at])
        outs.append(divide(total, mask).astype(BF16))
    att = jnp.concatenate(outs, axis=1)
    att_ref[...] = att
    emit(att, o_ref, (first,), 0)


def decode(late_ref, o_ref, m_ref, len_ref, cache, first, r1, r2, r3, slab, total_ref, below_ref, sems):
    steps = [(d, b) for d in range(DEC) for b in range(2)]

    def copy(d, b):
        at = pl.ds(b * 512, 512)
        return pltpu.make_async_copy(cache.at[d + 1, at], slab.at[d, at], sems.at[d, b])

    for d, b in steps:

        @pl.when(b * 512 < len_ref[d + 1])
        def _():
            copy(d, b).start()

    fresh = late_ref[:, 0:512]
    late = jnp.concatenate([query_of(late_ref[:, 512:640], h)[0] for h in range(4)], axis=1)
    own = row((16, 512)) == lane((16, 512)) // LANES
    queries = []
    for d in range(DEC):
        q = jnp.where(own, jnp.broadcast_to(late[d : d + 1], (16, 512)), 0.0)
        queries.append(q.astype(BF16))
        new = jnp.broadcast_to(fresh[d : d + 1], (16, 512))
        live = m_ref[2 * HALF + d : 2 * HALF + d + 1, 0:1]
        self_score = jnp.sum(q * new, axis=1, keepdims=True) + 1.0
        self_weight = (self_score * self_score + 1.0) * live
        total_ref[d] = self_weight.astype(BF16).astype(F32) * new
        below_ref[d] = jnp.broadcast_to(self_weight + 2.0 * (1.0 - live), (16, 128))
    for d, b in steps:

        @pl.when(b * 512 < len_ref[d + 1])
        def _():
            copy(d, b).wait()
            keys = slab[d, b * 512 : (b + 1) * 512, :]
            score = dot_nt(queries[d], keys) + 1.0
            position = b * 512 + lane((16, 512))
            weight = jnp.where(position < len_ref[d + 1], score * score + 1.0, 0.0)
            total_ref[d] += dot(weight.astype(BF16), keys)
            below_ref[d] += jnp.broadcast_to(jnp.sum(weight, axis=1, keepdims=True), (16, 128))

    decoded = jnp.zeros((16, 512), F32)
    for d in range(DEC):
        live = m_ref[2 * HALF + d : 2 * HALF + d + 1, 0:1]
        ratio = live * total_ref[d] / below_ref[d][:, 0:1]
        value = jnp.sum(jnp.where(own, ratio, 0.0), axis=0, keepdims=True)
        decoded = jnp.where(row((16, 512)) == d, jnp.broadcast_to(value, (16, 512)), decoded)
    place = gray(lax.axis_index("col"))
    for s, out in enumerate((first, r1, r2, r3)):
        part = dot(decoded.astype(BF16), o_ref[gray((place + 3 - s) & 3)])
        out[...] = jnp.concatenate(
            [part[0:DEC, t * 128 : (t + 1) * 128] for t in range(4)], axis=0
        ).astype(out.dtype)


def join(recv, part, new_ref, out):
    out[:BODY, :] = (recv[:BODY, :].astype(F32) + part[...]).astype(BF16)
    late = new_ref[...].astype(F32)
    if recv.shape[0] > BODY:
        late = late + recv[BODY:, :].astype(F32)
    out[BODY:, :] = late.astype(BF16)


def unpack_sum(recv, part, out, base):
    for t in range(3):
        at = slice(t * HALF, (t + 1) * HALF)
        out[base : base + HALF, t * 128 : (t + 1) * 128] = (recv[at, :].astype(F32) + part[at, :]).astype(BF16)
    tail = recv[TAIL:BODY, :].astype(F32) + part[TAIL:BODY, :]
    out[base : base + HALF // 2, 384:448] = tail[:, 0:64].astype(BF16)
    out[base + HALF // 2 : base + HALF, 384:448] = tail[:, 64:128].astype(BF16)


def finish_a(recv, part, back, own_late, out, late):
    unpack_sum(recv, part, out, 0)
    late[...] = recv[BODY:, :].astype(F32) + (back[...].astype(F32) + own_late[...])


def finish(done, late, recv, part, out):
    out[:HALF, :] = done[...]
    unpack_sum(recv, part, out, HALF)
    for t in range(4):
        width = 128 if t < 3 else 64
        rows = late[DEC * t : DEC * (t + 1), 0:width]
        out[SPAN_TOKENS:, t * 128 : t * 128 + width] = rows.astype(BF16)


def in_hbm(x):
    return pltpu.with_memory_space_constraint(x, pltpu.MemorySpace.HBM)


def after(value, *others):
    return lax.optimization_barrier((value, *others))[0]


def shards(hidden, norm_gain, qkv_weight, out_weight, cache, cached, token_mask):
    ring = [(gray(p), gray((p + 1) % 4)) for p in range(4)]

    def onward(x):
        return lax.ppermute(x, "col", ring)

    def across(x, k):
        return lax.ppermute(x, "row", [(i, i ^ k) for i in range(8)])

    a, b, own = call(
        pack,
        (shaped((BODY + EXTRA, 128)), shaped((BODY + EXTRA, 128)), shaped((WROWS, 128))),
        [HBM] * 4,
        scratch=[pltpu.VMEM(x.shape, BF16) for x in (hidden, norm_gain, qkv_weight, out_weight)]
        + [pltpu.SemaphoreType.DMA((4,))],
        nbytes=300_000,
        name="pack",
    )(*(in_hbm(x) for x in (hidden, norm_gain, qkv_weight, out_weight)))
    plane = [own] + [across(own, k) for k in (2, 4, 6)]

    def sums(x, name):
        return call(square_b, shaped((HALF + 16, 128), F32), [VMEM], flops=COST_SQ, nbytes=300_000, name=name)(x)

    a1, b1 = onward(a), onward(b)
    a2, b2 = onward(a1), onward(b1)
    s1, s2 = sums(b1, "square_b1"), sums(b2, "square_b2")
    a3 = after(onward(after(a2, s1)), s2, *plane[1:])
    a, b = [a, a1, a2, a3], [b, b1, b2, onward(b2)]
    blocks = [own, across(after(own, s2), 1)]
    for block in plane[1:]:
        blocks += [block, across(block, 1)]
    w, o = call(
        place_weights,
        (shaped((4, 512, 640)), shaped((4, 512, 512))),
        [VMEM] * 8,
        nbytes=300_000,
        name="place_weights",
    )(*blocks)
    na = call(norm_a, shaped((HALF, 2048)), [VMEM] * 4, flops=COST_X, nbytes=300_000, name="norm_a")(*a)
    ck, cv = call(
        prepare_cache,
        (shaped((1024, 512)), shaped((1024, 512))),
        [HBM, SMEM],
        scratch=[pltpu.VMEM((1024, 512), BF16), pltpu.SemaphoreType.DMA],
        nbytes=300_000,
        name="prepare_cache",
        mib=12,
    )(in_hbm(cache), cached)
    mask = jnp.broadcast_to(token_mask.astype(F32)[:, None], (token_mask.shape[0], 128))
    parts = (shaped((BODY, 128), F32),) * 3
    wide, wire = shaped((HALF, 512)), shaped((BODY, 128))
    first, *rest_a, ka, va = call(
        chunk_a,
        (wire, *parts, wide, wide),
        [VMEM] * 6,
        flops=COST_CA,
        nbytes=300_000,
        name="chunk_a",
        mib=20,
    )(na, w, o, ck, cv, mask)
    send_a = onward(first)
    first, att, late = call(
        chunk_b,
        (wire, wide, shaped((16, 640), F32)),
        [VMEM] * 17,
        scratch=[
            pltpu.VMEM((HALF + 16, 2048), BF16),
            pltpu.VMEM((HALF, 512), BF16),
            pltpu.VMEM((HALF, 512), BF16),
        ],
        flops=COST_CB,
        nbytes=300_000,
        name="chunk_b",
        mib=20,
    )(*b, s1, s2, *a, w, o, ck, cv, mask, ka, va)
    send_b = onward(first)
    own_b = call(hop_3, parts[0], [VMEM] * 2, flops=COST_E, nbytes=300_000, name="hop_3")(att, o)

    def hop(body, recv, name):
        return onward(call(body, wire, [VMEM] * 3, nbytes=300_000, name=name)(att, o, recv))

    few = shaped((EXTRA, 128), F32)
    back, *late = call(
        decode,
        (shaped((EXTRA, 128)), few, few, few),
        [VMEM] * 3 + [SMEM, HBM],
        scratch=[
            pltpu.VMEM((DEC, 1024, 512), BF16),
            pltpu.VMEM((DEC, 16, 512), F32),
            pltpu.VMEM((DEC, 16, 128), F32),
            pltpu.SemaphoreType.DMA((DEC, 2)),
        ],
        flops=COST_D,
        nbytes=300_000,
        name="decode",
        mib=12,
    )(late, o, mask, cached, in_hbm(cache))

    back = lax.ppermute(back, "col", [(gray((p + 1) % 4), gray(p)) for p in range(4)])

    def joined(recv, part, new, name):
        return call(join, shaped((BODY + EXTRA, 128)), [VMEM] * 3, nbytes=300_000, name=name)(recv, part, new)

    send_a = onward(joined(send_a, rest_a[0], late[0], "join_1"))
    send_b = hop(hop_1, send_b, "hop_1")
    send_a = onward(joined(after(send_a, back), rest_a[1], late[1], "join_2"))
    send_b = hop(hop_2, send_b, "hop_2")
    done = call(
        finish_a,
        (shaped((HALF, hidden.shape[1])), few),
        [VMEM] * 4,
        flops=COST_F,
        nbytes=300_000,
        name="finish_a",
    )(send_a, rest_a[2], back, late[2])
    return call(finish, shaped(hidden.shape), [VMEM] * 4, flops=COST_G, nbytes=300_000, name="finish")(
        *done, send_b, own_b
    )


def taylor(taylor_score):
    return 1.0 + taylor_score + 0.5 * taylor_score * taylor_score


def attend(projected, cache, cached, token_mask):
    rows = projected.shape[0]
    width = 2 * FEATURE_WIDTH + HDIM
    lanes = FEATURE_WIDTH + HDIM
    heads_here = projected.shape[1] // width
    parts = projected.reshape(rows, heads_here, width)
    query_rows = parts[:, :, :FEATURE_WIDTH]
    key_rows = parts[:, :, FEATURE_WIDTH : 2 * FEATURE_WIDTH]
    values = parts[:, :, 2 * FEATURE_WIDTH :]
    store = cache.reshape(cache.shape[0], cache.shape[1], heads_here, lanes)
    capacity = cache.shape[1]
    block = min(512, capacity)
    score_scale = FEATURE_WIDTH ** (-0.5)
    live = token_mask.astype(jnp.float32)
    prefill_query_rows = query_rows[:SPAN_TOKENS]
    prior_tokens = store[0]
    offset = cached[0]

    def span_step(index, carry):
        numer, denom = carry
        span_slice = lax.dynamic_slice_in_dim(prior_tokens, index * block, block, 0)
        position = index * block + lax.iota(jnp.int32, block)
        taylor_score = (
            jnp.einsum(
                "sue,pue->usp",
                prefill_query_rows,
                span_slice[:, :, :FEATURE_WIDTH],
                preferred_element_type=jnp.float32,
            )
            * score_scale
        )
        weight = taylor(taylor_score) * (position < offset).astype(jnp.float32)[None, None, :]
        numer = numer + jnp.einsum(
            "hqk,khd->hqd",
            weight.astype(jnp.bfloat16),
            span_slice[:, :, FEATURE_WIDTH:],
            preferred_element_type=jnp.float32,
        )
        return (numer, denom + jnp.sum(weight, axis=-1))

    start_numer = jnp.zeros((heads_here, SPAN_TOKENS, HDIM), jnp.float32)
    start_denom = jnp.zeros((heads_here, SPAN_TOKENS), jnp.float32)
    span_blocks = (offset + block - 1) // block
    numer, denom = lax.fori_loop(0, span_blocks, span_step, (start_numer, start_denom))
    taylor_score = (
        jnp.einsum(
            "sue,pue->usp",
            prefill_query_rows,
            key_rows[:SPAN_TOKENS],
            preferred_element_type=jnp.float32,
        )
        * score_scale
    )
    order = lax.iota(jnp.int32, SPAN_TOKENS)
    allowed = (order[None, :] <= order[:, None]).astype(jnp.float32) * live[:SPAN_TOKENS][None, :]
    weight = taylor(taylor_score) * allowed[None]
    numer = numer + jnp.einsum(
        "hqk,khd->hqd",
        weight.astype(jnp.bfloat16),
        values[:SPAN_TOKENS],
        preferred_element_type=jnp.float32,
    )
    denom = denom + jnp.sum(weight, axis=-1)
    decode_queries = query_rows[SPAN_TOKENS:]
    past = store[1:]
    counts = cached[1:]

    def decode_step(index, carry):
        dec_numer, dec_denom = carry
        span_slice = lax.dynamic_slice_in_dim(past, index * block, block, 1)
        position = index * block + lax.iota(jnp.int32, block)
        taylor_score = (
            jnp.einsum(
                "rhf,rkhf->rhk",
                decode_queries,
                span_slice[..., :FEATURE_WIDTH],
                preferred_element_type=jnp.float32,
            )
            * score_scale
        )
        seen = (position[None, :] < counts[:, None]).astype(jnp.float32)
        weight = taylor(taylor_score) * seen[:, None, :]
        dec_numer = dec_numer + jnp.einsum(
            "rhk,rkhd->rhd",
            weight.astype(jnp.bfloat16),
            span_slice[..., FEATURE_WIDTH:],
            preferred_element_type=jnp.float32,
        )
        return (dec_numer, dec_denom + jnp.sum(weight, axis=-1))

    first_numer = jnp.zeros((DEC, heads_here, HDIM), jnp.float32)
    first_denom = jnp.zeros((DEC, heads_here), jnp.float32)
    decode_blocks = (jnp.max(counts) + block - 1) // block
    dec_numer, dec_denom = lax.fori_loop(0, decode_blocks, decode_step, (first_numer, first_denom))
    taylor_score = (
        jnp.sum(
            decode_queries.astype(jnp.float32) * key_rows[SPAN_TOKENS:].astype(jnp.float32), axis=-1
        )
        * score_scale
    )
    weight = taylor(taylor_score) * live[SPAN_TOKENS:, None]
    dec_numer = dec_numer + weight.astype(jnp.bfloat16).astype(jnp.float32)[..., None] * values[
        SPAN_TOKENS:
    ].astype(jnp.float32)
    dec_denom = dec_denom + weight
    numer_all = jnp.concatenate([jnp.transpose(numer, (1, 0, 2)), dec_numer], axis=0)
    denom_all = jnp.concatenate([jnp.transpose(denom, (1, 0)), dec_denom], axis=0)
    result = live[:, None, None] * numer_all / (denom_all + 1.0 - live[:, None])[..., None]
    return result.astype(jnp.bfloat16).reshape(rows, heads_here * HDIM)


def plain_shards(hidden, norm_gain, qkv_weight, out_weight, cache, cached, token_mask):
    full, gain = (
        lax.all_gather(hidden, "col", axis=1, tiled=True),
        lax.all_gather(norm_gain, "col", axis=0, tiled=True),
    )
    wide = full.astype(jnp.float32)
    normed = (
        wide
        * lax.rsqrt(jnp.mean(wide * wide, axis=-1, keepdims=True) + 1e-06)
        * gain.astype(jnp.float32)
    )
    normed = normed.astype(jnp.bfloat16)
    projected = jnp.dot(
        normed,
        lax.all_gather(qkv_weight, "row", axis=0, tiled=True),
        preferred_element_type=jnp.float32,
    ).astype(jnp.bfloat16)
    attended = attend(projected, cache, cached, token_mask)
    terms = jnp.dot(
        attended,
        lax.all_gather(out_weight, "row", axis=1, tiled=True),
        preferred_element_type=jnp.float32,
    )
    mixed = lax.psum_scatter(terms, "col", scatter_dimension=1, tiled=True).astype(jnp.bfloat16)
    return mixed


def solution(mesh):
    in_specs = (
        P("row", "col"),
        P("col"),
        P("row", "col"),
        P("col", "row"),
        P("row", None, "col"),
        P("row"),
        P("row"),
    )
    out_specs = P("row", "col")
    body = shards if (mesh.shape["row"], mesh.shape["col"]) == (8, 4) else plain_shards
    return jax.shard_map(body, mesh=mesh, in_specs=in_specs, out_specs=out_specs, check_vma=False)
```

```python
import jax
import jax.numpy as jnp
from jax import lax
from jax.experimental import pallas as pl
from jax.experimental.pallas import tpu as pltpu
from jax.sharding import PartitionSpec as P

FEATURE_WIDTH = 16
HDIM = 112
SPAN_TOKENS = 512
DEC = 4
LANES = FEATURE_WIDTH + HDIM
F32 = jnp.float32
BF16 = jnp.bfloat16
HALF = SPAN_TOKENS // 2
VMEM = pl.BlockSpec(memory_space=pltpu.VMEM)
SMEM = pl.BlockSpec(memory_space=pltpu.SMEM)
HBM = pl.BlockSpec(memory_space=pltpu.MemorySpace.HBM)
TAIL = 3 * HALF
BODY = TAIL + HALF // 2
EXTRA = 16
QROWS = 224
OROWS = 448
WROWS = 4 * QROWS + 2 * OROWS
COST_X = 5_000_000_000
COST_SQ = 1_000_000_000
COST_CA = 100_000_000
COST_CB = 1_000_000_000
COST_F = 2_000_000_000
COST_G = 10_000_000
COST_D = 1_000_000
COST_E = 1_000_000


def gray(place):
    return place ^ (place >> 1)


def call(body, outs, in_specs, scratch=(), flops=0, nbytes=0, name=None, mib=8):
    return pl.pallas_call(
        body,
        out_shape=outs,
        in_specs=in_specs,
        out_specs=jax.tree.map(lambda _: VMEM, outs),
        scratch_shapes=scratch,
        cost_estimate=pl.CostEstimate(flops=flops, bytes_accessed=nbytes, transcendentals=0),
        compiler_params=pltpu.CompilerParams(vmem_limit_bytes=mib * 1024 * 1024),
        name=name,
    )


def shaped(shape, dtype=BF16):
    return jax.ShapeDtypeStruct(shape, dtype)


def dot(a, b):
    return jnp.dot(a, b, preferred_element_type=F32)


def dot_nt(a, b):
    return lax.dot_general(a, b, (((1,), (1,)), ((), ())), preferred_element_type=F32)


def lane(shape):
    return lax.broadcasted_iota(jnp.int32, shape, len(shape) - 1)


def row(shape):
    return lax.broadcasted_iota(jnp.int32, shape, 0)


def pack(hidden, gains, qkv, outs, a_ref, b_ref, w_ref, h_ref, g_ref, q_ref, o_ref, sems):
    pairs = ((hidden, h_ref), (gains, g_ref), (qkv, q_ref), (outs, o_ref))
    copies = [pltpu.make_async_copy(*pair, sems.at[n]) for n, pair in enumerate(pairs)]
    for copy in copies:
        copy.start()
    copies[0].wait()
    copies[1].wait()
    for ref, base in ((a_ref, 0), (b_ref, HALF)):
        for t in range(3):
            ref[t * HALF : (t + 1) * HALF, :] = h_ref[base : base + HALF, t * 128 : (t + 1) * 128]
        low = h_ref[base : base + HALF // 2, 384:448]
        high = h_ref[base + HALF // 2 : base + HALF, 384:448]
        ref[TAIL:BODY, :] = jnp.concatenate([low, high], axis=1)
        ref[BODY:, :] = jnp.zeros((EXTRA, 128), BF16)
    gain = g_ref[...].reshape(1, 448)
    for t in range(3):
        a_ref[BODY + t : BODY + t + 1, :] = gain[:, t * 128 : (t + 1) * 128]
        b_ref[BODY + DEC * t : BODY + DEC * (t + 1), :] = h_ref[SPAN_TOKENS:, t * 128 : (t + 1) * 128]
    last = gain[:, 384:448]
    a_ref[BODY + 3 : BODY + 4, :] = jnp.concatenate([last, last], axis=1)
    b_ref[BODY + 3 * DEC :, 0:64] = h_ref[SPAN_TOKENS:, 384:448]
    copies[2].wait()
    copies[3].wait()
    width = FEATURE_WIDTH + LANES
    for h in range(4):
        w_ref[h * QROWS : (h + 1) * QROWS, :] = q_ref[:, h * width + FEATURE_WIDTH : (h + 1) * width]
    at = 4 * QROWS
    w_ref[at : at + OROWS, :] = o_ref[:, 0:128]
    for side in range(2):
        pieces = [o_ref[side * QROWS : (side + 1) * QROWS, 128:224]]
        for h in (2 * side, 2 * side + 1):
            pieces.append(q_ref[:, h * width : h * width + FEATURE_WIDTH])
        rows = at + OROWS + side * QROWS
        w_ref[rows : rows + QROWS, :] = jnp.concatenate(pieces, axis=1)


def place_weights(*refs):
    blocks, (w_ref, o_ref) = refs[:8], refs[8:]
    me = lax.axis_index("row")
    at, late = 4 * QROWS, 4 * QROWS + OROWS

    def project_rows(block):
        queries = [block[late + s * QROWS : late + (s + 1) * QROWS, 96:128] for s in range(2)]
        queries.append(jnp.zeros((QROWS, 64), BF16))
        heads = [block[h * QROWS : (h + 1) * QROWS, :] for h in range(4)]
        return heads + [jnp.concatenate(queries, axis=1)]

    for core in range(2):

        @pl.when(me & 1 == core)
        def _():
            for k in range(4):
                j = (me >> 1) ^ k
                low, high = blocks[2 * k + core], blocks[2 * k + 1 - core]
                for t, tile in enumerate(project_rows(low)):
                    w_ref[j, 0:QROWS, t * 128 : (t + 1) * 128] = tile
                for t, tile in enumerate(project_rows(high)):
                    w_ref[j, QROWS : 2 * QROWS, t * 128 : (t + 1) * 128] = tile
                    w_ref[j, 448:512, t * 128 : (t + 1) * 128] = tile[160:QROWS, :]
                full = jnp.concatenate(
                    [low[at:late, :], low[late:, 0:96], high[at:late, :], high[late:, 0:96]], axis=1
                )
                full = jnp.concatenate([full, full[:, 384:448]], axis=1)
                for h in range(4):
                    o_ref[j, h * LANES : h * LANES + FEATURE_WIDTH, :] = jnp.zeros((FEATURE_WIDTH, 512), BF16)
                    o_ref[j, h * LANES + FEATURE_WIDTH : (h + 1) * LANES, :] = full[h * HDIM : (h + 1) * HDIM, :]


def as_keys(kv):
    return jnp.where(lane(kv.shape) % LANES == FEATURE_WIDTH, 1.0, kv).astype(BF16)


def as_values(kv, keep):
    ones = jnp.where(lane(kv.shape) % LANES < FEATURE_WIDTH, 1.0, kv)
    return jnp.where(keep, ones, 0.0).astype(BF16)


def prepare_cache(cache, len_ref, k_ref, v_ref, slab, sem):
    copy = pltpu.make_async_copy(cache.at[0], slab, sem)
    copy.start()
    copy.wait()
    kv = slab[...].astype(F32)
    k_ref[...] = as_keys(kv)
    v_ref[...] = as_values(kv, row(kv.shape) < len_ref[0])


def tiles_of(ref, rows):
    middle = lane((HALF // 2, 128)) < 64
    tail = ref[TAIL:BODY, :].astype(F32)
    tail = jnp.concatenate([jnp.where(middle, tail, 0.0), jnp.where(middle, 0.0, tail)], axis=0)
    tiles = [ref[t * HALF : (t + 1) * HALF, :].astype(F32) for t in range(3)] + [tail]
    if rows > HALF:
        extra = ref[BODY:, :].astype(F32)
        late = [extra[DEC * t : DEC * (t + 1), :] for t in range(4)]
        zeros = jnp.zeros((16 - DEC, 128), F32)
        tiles = [jnp.concatenate(parts + (zeros,), axis=0) for parts in zip(tiles, late)]
    return tiles


def squares(tiles):
    total = tiles[0] * tiles[0]
    for tile in tiles[1:]:
        total = total + tile * tile
    return total


def square_b(ref, out):
    out[...] = squares(tiles_of(ref, HALF + 16))


def norm(blocks, gain_ref, sums, out_ref, rows):
    pieces = [tiles_of(ref, rows) for ref in blocks]
    total = None
    for k, tiles in enumerate(pieces):
        part = sums[k][...] if k in sums else squares(tiles)
        total = part if total is None else total + part
    mean = jnp.sum(total, axis=1, keepdims=True) * (1.0 / 1792.0)
    scale = jnp.broadcast_to(lax.rsqrt(mean + 1e-06), (rows, 128))
    for k, tiles in enumerate(pieces):
        for t, tile in enumerate(tiles):
            gain = gain_ref[k][BODY + t : BODY + t + 1, :].astype(F32)
            out_ref[:, k * 512 + t * 128 : k * 512 + (t + 1) * 128] = (tile * scale * gain).astype(BF16)


def norm_a(a0, a1, a2, a3, out):
    norm((a0, a1, a2, a3), (a0, a1, a2, a3), {}, out, HALF)


def project(normed, w_ref):
    place = gray(lax.axis_index("col"))
    total = None
    for k in range(4):
        term = dot(normed[:, k * 512 : (k + 1) * 512], w_ref[gray((place + 4 - k) & 3)])
        total = term if total is None else total + term
    total = total.astype(BF16).astype(F32)
    return total[:, 0:512], total[:, 512:640]


def query_of(queries, h):
    q = pltpu.roll(queries, (128 - FEATURE_WIDTH * h) % 128, 1) if h else queries
    at = lane(q.shape)
    return jnp.where(at < FEATURE_WIDTH, q * FEATURE_WIDTH**-0.5, 0.0), at == FEATURE_WIDTH


def weigh(scores, keep=None):
    weight = scores * scores + 1.0
    if keep is not None:
        weight = jnp.where(keep, weight, 0.0)
    return weight.astype(BF16)


def divide(total, mask):
    below = jnp.broadcast_to(total[:, 0:1], total.shape) + 2.0 * (1.0 - mask)
    return mask * total / below


def emit(att, o_ref, outs, start, recv=None):
    place = gray(lax.axis_index("col"))
    middle = lane((HALF // 2, 128)) < 64
    for s, out in enumerate(outs, start):
        part = dot(att, o_ref[gray((place + 3 - s) & 3)])
        tiles = [part[:, t * 128 : (t + 1) * 128] for t in range(3)]
        last = part[:, 384:512]
        tiles.append(jnp.where(middle, last[: HALF // 2], last[HALF // 2 :]))
        for t, tile in enumerate(tiles):
            at = slice(t * HALF, t * HALF + tile.shape[0])
            if recv is not None:
                tile = tile + recv[at, :].astype(F32)
            out[at, :] = tile.astype(out.dtype)


def hop_1(att_ref, o_ref, recv, late, out):
    emit(att_ref[...], o_ref, (out,), 1, recv)
    out[BODY:, :] = late[...].astype(BF16)


def hop_2(att_ref, o_ref, recv, late, out):
    emit(att_ref[...], o_ref, (out,), 2, recv)
    out[BODY:, :] = (recv[BODY:, :].astype(F32) + late[...]).astype(BF16)


def hop_3(att_ref, o_ref, out):
    emit(att_ref[...], o_ref, (out,), 3)


def chunk_a(normed, w_ref, o_ref, ck_ref, cv_ref, m_ref, first, r1, r2, r3, ka_ref, va_ref):
    kv, queries = project(normed, w_ref)
    mask = m_ref[0:HALF, :]
    ka_ref[...] = as_keys(kv)
    va_ref[...] = as_values(kv, jnp.concatenate([mask] * 4, axis=1) > 0.0)
    causal = lane((HALF, HALF)) <= row((HALF, HALF))
    outs = []
    for h in range(4):
        at = slice(h * LANES, (h + 1) * LANES)
        q, one = query_of(queries, h)
        q = jnp.where(one, 1.0, q).astype(BF16)
        total = dot(weigh(dot_nt(q, ka_ref[:, at]), causal), va_ref[:, at])
        for b in range(2):
            keys = slice(b * 512, (b + 1) * 512)
            total += dot(weigh(dot_nt(q, ck_ref[keys, at])), cv_ref[keys, at])
        outs.append(divide(total, mask).astype(BF16))
    emit(jnp.concatenate(outs, axis=1), o_ref, (first, r1, r2, r3), 0)


def chunk_b(
    b0, b1, b2, b3, s1, s2, a0, a1, a2, a3, w_ref, o_ref, ck_ref, cv_ref, m_ref, ka_ref, va_ref, first, att_ref, late_ref, normed, kb, vb
):
    norm((b0, b1, b2, b3), (a0, a1, a2, a3), {1: s1, 2: s2}, normed, HALF + 16)
    kv, queries = project(normed, w_ref)
    late_ref[:, 0:512] = kv[HALF:]
    late_ref[:, 512:640] = queries[HALF:]
    kv, queries = kv[:HALF], queries[:HALF]
    mask = m_ref[HALF : 2 * HALF, :]
    kb[...] = as_keys(kv)
    vb[...] = as_values(kv, jnp.concatenate([mask] * 4, axis=1) > 0.0)
    causal = lane((HALF, HALF)) <= row((HALF, HALF))
    outs = []
    for h in range(4):
        at = slice(h * LANES, (h + 1) * LANES)
        q, one = query_of(queries, h)
        q = jnp.where(one, 1.0, q).astype(BF16)
        total = dot(weigh(dot_nt(q, kb[:, at]), causal), vb[:, at])
        total += dot(weigh(dot_nt(q, ka_ref[:, at])), va_ref[:, at])
        for b in range(2):
            keys = slice(b * 512, (b + 1) * 512)
            total += dot(weigh(dot_nt(q, ck_ref[keys, at])), cv_ref[keys, at])
        outs.append(divide(total, mask).astype(BF16))
    att = jnp.concatenate(outs, axis=1)
    att_ref[...] = att
    emit(att, o_ref, (first,), 0)


def decode(late_ref, o_ref, m_ref, len_ref, cache, first, r1, r2, r3, slab, total_ref, below_ref, sems):
    steps = [(d, b) for d in range(DEC) for b in range(2)]

    def copy(d, b):
        at = pl.ds(b * 512, 512)
        return pltpu.make_async_copy(cache.at[d + 1, at], slab.at[d, at], sems.at[d, b])

    for d, b in steps:

        @pl.when(b * 512 < len_ref[d + 1])
        def _():
            copy(d, b).start()

    fresh = late_ref[:, 0:512]
    late = jnp.concatenate([query_of(late_ref[:, 512:640], h)[0] for h in range(4)], axis=1)
    own = row((16, 512)) == lane((16, 512)) // LANES
    queries = []
    for d in range(DEC):
        q = jnp.where(own, jnp.broadcast_to(late[d : d + 1], (16, 512)), 0.0)
        queries.append(q.astype(BF16))
        new = jnp.broadcast_to(fresh[d : d + 1], (16, 512))
        live = m_ref[2 * HALF + d : 2 * HALF + d + 1, 0:1]
        self_score = jnp.sum(q * new, axis=1, keepdims=True) + 1.0
        self_weight = (self_score * self_score + 1.0) * live
        total_ref[d] = self_weight.astype(BF16).astype(F32) * new
        below_ref[d] = jnp.broadcast_to(self_weight + 2.0 * (1.0 - live), (16, 128))
    for d, b in steps:

        @pl.when(b * 512 < len_ref[d + 1])
        def _():
            copy(d, b).wait()
            keys = slab[d, b * 512 : (b + 1) * 512, :]
            score = dot_nt(queries[d], keys) + 1.0
            position = b * 512 + lane((16, 512))
            weight = jnp.where(position < len_ref[d + 1], score * score + 1.0, 0.0)
            total_ref[d] += dot(weight.astype(BF16), keys)
            below_ref[d] += jnp.broadcast_to(jnp.sum(weight, axis=1, keepdims=True), (16, 128))

    decoded = jnp.zeros((16, 512), F32)
    for d in range(DEC):
        live = m_ref[2 * HALF + d : 2 * HALF + d + 1, 0:1]
        ratio = live * total_ref[d] / below_ref[d][:, 0:1]
        value = jnp.sum(jnp.where(own, ratio, 0.0), axis=0, keepdims=True)
        decoded = jnp.where(row((16, 512)) == d, jnp.broadcast_to(value, (16, 512)), decoded)
    place = gray(lax.axis_index("col"))
    for s, out in enumerate((first, r1, r2, r3)):
        part = dot(decoded.astype(BF16), o_ref[gray((place + 3 - s) & 3)])
        out[...] = jnp.concatenate(
            [part[0:DEC, t * 128 : (t + 1) * 128] for t in range(4)], axis=0
        ).astype(out.dtype)


def unpack_sum(recv, part, out, base):
    for t in range(3):
        at = slice(t * HALF, (t + 1) * HALF)
        out[base : base + HALF, t * 128 : (t + 1) * 128] = (recv[at, :].astype(F32) + part[at, :]).astype(BF16)
    tail = recv[TAIL:BODY, :].astype(F32) + part[TAIL:BODY, :]
    out[base : base + HALF // 2, 384:448] = tail[:, 0:64].astype(BF16)
    out[base + HALF // 2 : base + HALF, 384:448] = tail[:, 64:128].astype(BF16)


def finish_a(recv, part, out):
    unpack_sum(recv, part, out, 0)


def finish(done, recv, part, back, own_late, out):
    out[:HALF, :] = done[...]
    unpack_sum(recv, part, out, HALF)
    late = recv[BODY:, :].astype(F32) + (back[...].astype(F32) + own_late[...])
    for t in range(4):
        width = 128 if t < 3 else 64
        rows = late[DEC * t : DEC * (t + 1), 0:width]
        out[SPAN_TOKENS:, t * 128 : t * 128 + width] = rows.astype(BF16)


def in_hbm(x):
    return pltpu.with_memory_space_constraint(x, pltpu.MemorySpace.HBM)


def after(value, *others):
    return lax.optimization_barrier((value, *others))[0]


def shards(hidden, norm_gain, qkv_weight, out_weight, cache, cached, token_mask):
    ring = [(gray(p), gray((p + 1) % 4)) for p in range(4)]

    def onward(x):
        return lax.ppermute(x, "col", ring)

    def across(x, k):
        return lax.ppermute(x, "row", [(i, i ^ k) for i in range(8)])

    a, b, own = call(
        pack,
        (shaped((BODY + EXTRA, 128)), shaped((BODY + EXTRA, 128)), shaped((WROWS, 128))),
        [HBM] * 4,
        scratch=[pltpu.VMEM(x.shape, BF16) for x in (hidden, norm_gain, qkv_weight, out_weight)]
        + [pltpu.SemaphoreType.DMA((4,))],
        nbytes=300_000,
        name="pack",
    )(*(in_hbm(x) for x in (hidden, norm_gain, qkv_weight, out_weight)))
    plane = [own] + [across(own, k) for k in (2, 4, 6)]

    def sums(x, name):
        return call(square_b, shaped((HALF + 16, 128), F32), [VMEM], flops=COST_SQ, nbytes=300_000, name=name)(x)

    a1, b1 = onward(a), onward(b)
    a2, b2 = onward(a1), onward(b1)
    s1, s2 = sums(b1, "square_b1"), sums(b2, "square_b2")
    a3 = after(onward(after(a2, s1)), s2, *plane[1:])
    a, b = [a, a1, a2, a3], [b, b1, b2, onward(b2)]
    blocks = [own, across(after(own, s2), 1)]
    for block in plane[1:]:
        blocks += [block, across(block, 1)]
    w, o = call(
        place_weights,
        (shaped((4, 512, 640)), shaped((4, 512, 512))),
        [VMEM] * 8,
        nbytes=300_000,
        name="place_weights",
    )(*blocks)
    na = call(norm_a, shaped((HALF, 2048)), [VMEM] * 4, flops=COST_X, nbytes=300_000, name="norm_a")(*a)
    ck, cv = call(
        prepare_cache,
        (shaped((1024, 512)), shaped((1024, 512))),
        [HBM, SMEM],
        scratch=[pltpu.VMEM((1024, 512), BF16), pltpu.SemaphoreType.DMA],
        nbytes=300_000,
        name="prepare_cache",
        mib=12,
    )(in_hbm(cache), cached)
    mask = jnp.broadcast_to(token_mask.astype(F32)[:, None], (token_mask.shape[0], 128))
    parts = (shaped((BODY, 128), F32),) * 3
    wide, wire = shaped((HALF, 512)), shaped((BODY, 128))
    first, *rest_a, ka, va = call(
        chunk_a,
        (wire, *parts, wide, wide),
        [VMEM] * 6,
        flops=COST_CA,
        nbytes=300_000,
        name="chunk_a",
        mib=20,
    )(na, w, o, ck, cv, mask)
    send_a = onward(first)
    first, att, late = call(
        chunk_b,
        (wire, wide, shaped((16, 640), F32)),
        [VMEM] * 17,
        scratch=[
            pltpu.VMEM((HALF + 16, 2048), BF16),
            pltpu.VMEM((HALF, 512), BF16),
            pltpu.VMEM((HALF, 512), BF16),
        ],
        flops=COST_CB,
        nbytes=300_000,
        name="chunk_b",
        mib=20,
    )(*b, s1, s2, *a, w, o, ck, cv, mask, ka, va)
    send_b = onward(first)
    own_b = call(hop_3, parts[0], [VMEM] * 2, flops=COST_E, nbytes=300_000, name="hop_3")(att, o)

    few = shaped((EXTRA, 128), F32)
    back, *late = call(
        decode,
        (shaped((EXTRA, 128)), few, few, few),
        [VMEM] * 3 + [SMEM, HBM],
        scratch=[
            pltpu.VMEM((DEC, 1024, 512), BF16),
            pltpu.VMEM((DEC, 16, 512), F32),
            pltpu.VMEM((DEC, 16, 128), F32),
            pltpu.SemaphoreType.DMA((DEC, 2)),
        ],
        flops=COST_D,
        nbytes=300_000,
        name="decode",
        mib=12,
    )(late, o, mask, cached, in_hbm(cache))

    back = lax.ppermute(back, "col", [(gray((p + 1) % 4), gray(p)) for p in range(4)])

    def hop(body, recv, new, name):
        return onward(
            call(body, shaped((BODY + EXTRA, 128)), [VMEM] * 4, nbytes=300_000, name=name)(att, o, recv, new)
        )

    send_a = onward((send_a.astype(F32) + rest_a[0]).astype(BF16))
    send_b = hop(hop_1, send_b, late[0], "hop_1")
    send_a = onward((send_a.astype(F32) + rest_a[1]).astype(BF16))
    send_b = hop(hop_2, send_b, late[1], "hop_2")
    done = call(
        finish_a, shaped((HALF, hidden.shape[1])), [VMEM] * 2, flops=COST_F, nbytes=300_000, name="finish_a"
    )(send_a, rest_a[2])
    return call(finish, shaped(hidden.shape), [VMEM] * 5, flops=COST_G, nbytes=300_000, name="finish")(
        done, send_b, own_b, back, late[2]
    )


def taylor(taylor_score):
    return 1.0 + taylor_score + 0.5 * taylor_score * taylor_score


def attend(projected, cache, cached, token_mask):
    rows = projected.shape[0]
    width = 2 * FEATURE_WIDTH + HDIM
    lanes = FEATURE_WIDTH + HDIM
    heads_here = projected.shape[1] // width
    parts = projected.reshape(rows, heads_here, width)
    query_rows = parts[:, :, :FEATURE_WIDTH]
    key_rows = parts[:, :, FEATURE_WIDTH : 2 * FEATURE_WIDTH]
    values = parts[:, :, 2 * FEATURE_WIDTH :]
    store = cache.reshape(cache.shape[0], cache.shape[1], heads_here, lanes)
    capacity = cache.shape[1]
    block = min(512, capacity)
    score_scale = FEATURE_WIDTH ** (-0.5)
    live = token_mask.astype(jnp.float32)
    prefill_query_rows = query_rows[:SPAN_TOKENS]
    prior_tokens = store[0]
    offset = cached[0]

    def span_step(index, carry):
        numer, denom = carry
        span_slice = lax.dynamic_slice_in_dim(prior_tokens, index * block, block, 0)
        position = index * block + lax.iota(jnp.int32, block)
        taylor_score = (
            jnp.einsum(
                "sue,pue->usp",
                prefill_query_rows,
                span_slice[:, :, :FEATURE_WIDTH],
                preferred_element_type=jnp.float32,
            )
            * score_scale
        )
        weight = taylor(taylor_score) * (position < offset).astype(jnp.float32)[None, None, :]
        numer = numer + jnp.einsum(
            "hqk,khd->hqd",
            weight.astype(jnp.bfloat16),
            span_slice[:, :, FEATURE_WIDTH:],
            preferred_element_type=jnp.float32,
        )
        return (numer, denom + jnp.sum(weight, axis=-1))

    start_numer = jnp.zeros((heads_here, SPAN_TOKENS, HDIM), jnp.float32)
    start_denom = jnp.zeros((heads_here, SPAN_TOKENS), jnp.float32)
    span_blocks = (offset + block - 1) // block
    numer, denom = lax.fori_loop(0, span_blocks, span_step, (start_numer, start_denom))
    taylor_score = (
        jnp.einsum(
            "sue,pue->usp",
            prefill_query_rows,
            key_rows[:SPAN_TOKENS],
            preferred_element_type=jnp.float32,
        )
        * score_scale
    )
    order = lax.iota(jnp.int32, SPAN_TOKENS)
    allowed = (order[None, :] <= order[:, None]).astype(jnp.float32) * live[:SPAN_TOKENS][None, :]
    weight = taylor(taylor_score) * allowed[None]
    numer = numer + jnp.einsum(
        "hqk,khd->hqd",
        weight.astype(jnp.bfloat16),
        values[:SPAN_TOKENS],
        preferred_element_type=jnp.float32,
    )
    denom = denom + jnp.sum(weight, axis=-1)
    decode_queries = query_rows[SPAN_TOKENS:]
    past = store[1:]
    counts = cached[1:]

    def decode_step(index, carry):
        dec_numer, dec_denom = carry
        span_slice = lax.dynamic_slice_in_dim(past, index * block, block, 1)
        position = index * block + lax.iota(jnp.int32, block)
        taylor_score = (
            jnp.einsum(
                "rhf,rkhf->rhk",
                decode_queries,
                span_slice[..., :FEATURE_WIDTH],
                preferred_element_type=jnp.float32,
            )
            * score_scale
        )
        seen = (position[None, :] < counts[:, None]).astype(jnp.float32)
        weight = taylor(taylor_score) * seen[:, None, :]
        dec_numer = dec_numer + jnp.einsum(
            "rhk,rkhd->rhd",
            weight.astype(jnp.bfloat16),
            span_slice[..., FEATURE_WIDTH:],
            preferred_element_type=jnp.float32,
        )
        return (dec_numer, dec_denom + jnp.sum(weight, axis=-1))

    first_numer = jnp.zeros((DEC, heads_here, HDIM), jnp.float32)
    first_denom = jnp.zeros((DEC, heads_here), jnp.float32)
    decode_blocks = (jnp.max(counts) + block - 1) // block
    dec_numer, dec_denom = lax.fori_loop(0, decode_blocks, decode_step, (first_numer, first_denom))
    taylor_score = (
        jnp.sum(
            decode_queries.astype(jnp.float32) * key_rows[SPAN_TOKENS:].astype(jnp.float32), axis=-1
        )
        * score_scale
    )
    weight = taylor(taylor_score) * live[SPAN_TOKENS:, None]
    dec_numer = dec_numer + weight.astype(jnp.bfloat16).astype(jnp.float32)[..., None] * values[
        SPAN_TOKENS:
    ].astype(jnp.float32)
    dec_denom = dec_denom + weight
    numer_all = jnp.concatenate([jnp.transpose(numer, (1, 0, 2)), dec_numer], axis=0)
    denom_all = jnp.concatenate([jnp.transpose(denom, (1, 0)), dec_denom], axis=0)
    result = live[:, None, None] * numer_all / (denom_all + 1.0 - live[:, None])[..., None]
    return result.astype(jnp.bfloat16).reshape(rows, heads_here * HDIM)


def plain_shards(hidden, norm_gain, qkv_weight, out_weight, cache, cached, token_mask):
    full, gain = (
        lax.all_gather(hidden, "col", axis=1, tiled=True),
        lax.all_gather(norm_gain, "col", axis=0, tiled=True),
    )
    wide = full.astype(jnp.float32)
    normed = (
        wide
        * lax.rsqrt(jnp.mean(wide * wide, axis=-1, keepdims=True) + 1e-06)
        * gain.astype(jnp.float32)
    )
    normed = normed.astype(jnp.bfloat16)
    projected = jnp.dot(
        normed,
        lax.all_gather(qkv_weight, "row", axis=0, tiled=True),
        preferred_element_type=jnp.float32,
    ).astype(jnp.bfloat16)
    attended = attend(projected, cache, cached, token_mask)
    terms = jnp.dot(
        attended,
        lax.all_gather(out_weight, "row", axis=1, tiled=True),
        preferred_element_type=jnp.float32,
    )
    mixed = lax.psum_scatter(terms, "col", scatter_dimension=1, tiled=True).astype(jnp.bfloat16)
    return mixed


def solution(mesh):
    in_specs = (
        P("row", "col"),
        P("col"),
        P("row", "col"),
        P("col", "row"),
        P("row", None, "col"),
        P("row"),
        P("row"),
    )
    out_specs = P("row", "col")
    body = shards if (mesh.shape["row"], mesh.shape["col"]) == (8, 4) else plain_shards
    return jax.shard_map(body, mesh=mesh, in_specs=in_specs, out_specs=out_specs, check_vma=False)
```

```python
import jax
import jax.numpy as jnp
from jax import lax
from jax.experimental import pallas as pl
from jax.experimental.pallas import tpu as pltpu
from jax.sharding import PartitionSpec as P

FEATURE_WIDTH = 16
HDIM = 112
SPAN_TOKENS = 512
DEC = 4
LANES = FEATURE_WIDTH + HDIM
F32 = jnp.float32
BF16 = jnp.bfloat16
HALF = SPAN_TOKENS // 2
VMEM = pl.BlockSpec(memory_space=pltpu.VMEM)
SMEM = pl.BlockSpec(memory_space=pltpu.SMEM)
HBM = pl.BlockSpec(memory_space=pltpu.MemorySpace.HBM)
TAIL = 3 * HALF
BODY = TAIL + HALF // 2
EXTRA = 16
QROWS = 224
OROWS = 448
WROWS = 4 * QROWS + 2 * OROWS
COST_X = 5_000_000_000
COST_SQ = 1_000_000_000
COST_CA = 100_000_000
COST_CB = 1_000_000_000
COST_F = 2_000_000_000
COST_G = 10_000_000
COST_D = 1_000_000
COST_E = 1_000_000


def gray(place):
    return place ^ (place >> 1)


def call(body, outs, in_specs, scratch=(), flops=0, nbytes=0, name=None, mib=8):
    return pl.pallas_call(
        body,
        out_shape=outs,
        in_specs=in_specs,
        out_specs=jax.tree.map(lambda _: VMEM, outs),
        scratch_shapes=scratch,
        cost_estimate=pl.CostEstimate(flops=flops, bytes_accessed=nbytes, transcendentals=0),
        compiler_params=pltpu.CompilerParams(vmem_limit_bytes=mib * 1024 * 1024),
        name=name,
    )


def shaped(shape, dtype=BF16):
    return jax.ShapeDtypeStruct(shape, dtype)


def dot(a, b):
    return jnp.dot(a, b, preferred_element_type=F32)


def dot_nt(a, b):
    return lax.dot_general(a, b, (((1,), (1,)), ((), ())), preferred_element_type=F32)


def lane(shape):
    return lax.broadcasted_iota(jnp.int32, shape, len(shape) - 1)


def row(shape):
    return lax.broadcasted_iota(jnp.int32, shape, 0)


def pack(hidden, gains, qkv, outs, a_ref, b_ref, w_ref, h_ref, g_ref, q_ref, o_ref, sems):
    pairs = ((hidden, h_ref), (gains, g_ref), (qkv, q_ref), (outs, o_ref))
    copies = [pltpu.make_async_copy(*pair, sems.at[n]) for n, pair in enumerate(pairs)]
    for copy in copies:
        copy.start()
    copies[0].wait()
    copies[1].wait()
    for ref, base in ((a_ref, 0), (b_ref, HALF)):
        for t in range(3):
            ref[t * HALF : (t + 1) * HALF, :] = h_ref[base : base + HALF, t * 128 : (t + 1) * 128]
        low = h_ref[base : base + HALF // 2, 384:448]
        high = h_ref[base + HALF // 2 : base + HALF, 384:448]
        ref[TAIL:BODY, :] = jnp.concatenate([low, high], axis=1)
        ref[BODY:, :] = jnp.zeros((ref.shape[0] - BODY, 128), BF16)
    gain = g_ref[...].reshape(1, 448)
    for t in range(3):
        a_ref[BODY + t : BODY + t + 1, :] = gain[:, t * 128 : (t + 1) * 128]
        b_ref[BODY + DEC * t : BODY + DEC * (t + 1), :] = h_ref[SPAN_TOKENS:, t * 128 : (t + 1) * 128]
    last = gain[:, 384:448]
    a_ref[BODY + 3 : BODY + 4, :] = jnp.concatenate([last, last], axis=1)
    b_ref[BODY + 3 * DEC :, 0:64] = h_ref[SPAN_TOKENS:, 384:448]
    copies[2].wait()
    copies[3].wait()
    width = FEATURE_WIDTH + LANES
    for h in range(4):
        w_ref[h * QROWS : (h + 1) * QROWS, :] = q_ref[:, h * width + FEATURE_WIDTH : (h + 1) * width]
    at = 4 * QROWS
    w_ref[at : at + OROWS, :] = o_ref[:, 0:128]
    for side in range(2):
        pieces = [o_ref[side * QROWS : (side + 1) * QROWS, 128:224]]
        for h in (2 * side, 2 * side + 1):
            pieces.append(q_ref[:, h * width : h * width + FEATURE_WIDTH])
        rows = at + OROWS + side * QROWS
        w_ref[rows : rows + QROWS, :] = jnp.concatenate(pieces, axis=1)


def place_weights(*refs):
    blocks, (w_ref, o_ref) = refs[:8], refs[8:]
    me = lax.axis_index("row")
    at, late = 4 * QROWS, 4 * QROWS + OROWS

    def project_rows(block):
        queries = [block[late + s * QROWS : late + (s + 1) * QROWS, 96:128] for s in range(2)]
        queries.append(jnp.zeros((QROWS, 64), BF16))
        heads = [block[h * QROWS : (h + 1) * QROWS, :] for h in range(4)]
        return heads + [jnp.concatenate(queries, axis=1)]

    for core in range(2):

        @pl.when(me & 1 == core)
        def _():
            for k in range(4):
                j = (me >> 1) ^ k
                low, high = blocks[2 * k + core], blocks[2 * k + 1 - core]
                for t, tile in enumerate(project_rows(low)):
                    w_ref[j, 0:QROWS, t * 128 : (t + 1) * 128] = tile
                for t, tile in enumerate(project_rows(high)):
                    w_ref[j, QROWS : 2 * QROWS, t * 128 : (t + 1) * 128] = tile
                    w_ref[j, 448:512, t * 128 : (t + 1) * 128] = tile[160:QROWS, :]
                full = jnp.concatenate(
                    [low[at:late, :], low[late:, 0:96], high[at:late, :], high[late:, 0:96]], axis=1
                )
                full = jnp.concatenate([full, full[:, 384:448]], axis=1)
                for h in range(4):
                    o_ref[j, h * LANES : h * LANES + FEATURE_WIDTH, :] = jnp.zeros((FEATURE_WIDTH, 512), BF16)
                    o_ref[j, h * LANES + FEATURE_WIDTH : (h + 1) * LANES, :] = full[h * HDIM : (h + 1) * HDIM, :]


def as_keys(kv):
    return jnp.where(lane(kv.shape) % LANES == FEATURE_WIDTH, 1.0, kv).astype(BF16)


def as_values(kv, keep):
    ones = jnp.where(lane(kv.shape) % LANES < FEATURE_WIDTH, 1.0, kv)
    return jnp.where(keep, ones, 0.0).astype(BF16)


def prepare_cache(cache, len_ref, k_ref, v_ref, slab, sem):
    copy = pltpu.make_async_copy(cache.at[0], slab, sem)
    copy.start()
    copy.wait()
    kv = slab[...].astype(F32)
    k_ref[...] = as_keys(kv)
    v_ref[...] = as_values(kv, row(kv.shape) < len_ref[0])


def tiles_of(ref, rows):
    middle = lane((HALF // 2, 128)) < 64
    tail = ref[TAIL:BODY, :].astype(F32)
    tail = jnp.concatenate([jnp.where(middle, tail, 0.0), jnp.where(middle, 0.0, tail)], axis=0)
    tiles = [ref[t * HALF : (t + 1) * HALF, :].astype(F32) for t in range(3)] + [tail]
    if rows > HALF:
        extra = ref[BODY:, :].astype(F32)
        late = [extra[DEC * t : DEC * (t + 1), :] for t in range(4)]
        zeros = jnp.zeros((16 - DEC, 128), F32)
        tiles = [jnp.concatenate(parts + (zeros,), axis=0) for parts in zip(tiles, late)]
    return tiles


def squares(tiles):
    total = tiles[0] * tiles[0]
    for tile in tiles[1:]:
        total = total + tile * tile
    return total


def square_b(ref, out):
    out[...] = squares(tiles_of(ref, HALF + 16))


def norm(blocks, gain_ref, sums, out_ref, rows):
    pieces = [tiles_of(ref, rows) for ref in blocks]
    total = None
    for k, tiles in enumerate(pieces):
        part = sums[k][...] if k in sums else squares(tiles)
        total = part if total is None else total + part
    mean = jnp.sum(total, axis=1, keepdims=True) * (1.0 / 1792.0)
    scale = jnp.broadcast_to(lax.rsqrt(mean + 1e-06), (rows, 128))
    for k, tiles in enumerate(pieces):
        for t, tile in enumerate(tiles):
            gain = gain_ref[k][BODY + t : BODY + t + 1, :].astype(F32)
            out_ref[:, k * 512 + t * 128 : k * 512 + (t + 1) * 128] = (tile * scale * gain).astype(BF16)


def norm_a(a0, a1, a2, a3, out):
    norm((a0, a1, a2, a3), (a0, a1, a2, a3), {}, out, HALF)


def project(normed, w_ref):
    place = gray(lax.axis_index("col"))
    total = None
    for k in range(4):
        term = dot(normed[:, k * 512 : (k + 1) * 512], w_ref[gray((place + 4 - k) & 3)])
        total = term if total is None else total + term
    total = total.astype(BF16).astype(F32)
    return total[:, 0:512], total[:, 512:640]


def query_of(queries, h):
    q = pltpu.roll(queries, (128 - FEATURE_WIDTH * h) % 128, 1) if h else queries
    at = lane(q.shape)
    return jnp.where(at < FEATURE_WIDTH, q * FEATURE_WIDTH**-0.5, 0.0), at == FEATURE_WIDTH


def weigh(scores, keep=None):
    weight = scores * scores + 1.0
    if keep is not None:
        weight = jnp.where(keep, weight, 0.0)
    return weight.astype(BF16)


def divide(total, mask):
    below = jnp.broadcast_to(total[:, 0:1], total.shape) + 2.0 * (1.0 - mask)
    return mask * total / below


def emit(att, o_ref, outs, start, recv=None):
    place = gray(lax.axis_index("col"))
    middle = lane((HALF // 2, 128)) < 64
    for s, out in enumerate(outs, start):
        part = dot(att, o_ref[gray((place + 3 - s) & 3)])
        tiles = [part[:, t * 128 : (t + 1) * 128] for t in range(3)]
        last = part[:, 384:512]
        tiles.append(jnp.where(middle, last[: HALF // 2], last[HALF // 2 :]))
        for t, tile in enumerate(tiles):
            at = slice(t * HALF, t * HALF + tile.shape[0])
            if recv is not None:
                tile = tile + recv[at, :].astype(F32)
            out[at, :] = tile.astype(out.dtype)


def hop_1(att_ref, o_ref, recv, late, out):
    emit(att_ref[...], o_ref, (out,), 1, recv)
    out[BODY:, :] = late[...].astype(BF16)


def hop_2(att_ref, o_ref, recv, late, out):
    emit(att_ref[...], o_ref, (out,), 2, recv)
    out[BODY:, :] = (recv[BODY:, :].astype(F32) + late[...]).astype(BF16)


def hop_3(att_ref, o_ref, out):
    emit(att_ref[...], o_ref, (out,), 3)


def chunk_a(normed, w_ref, o_ref, ck_ref, cv_ref, m_ref, first, r1, r2, r3, ka_ref, va_ref):
    kv, queries = project(normed, w_ref)
    mask = m_ref[0:HALF, :]
    ka_ref[...] = as_keys(kv)
    va_ref[...] = as_values(kv, jnp.concatenate([mask] * 4, axis=1) > 0.0)
    causal = lane((HALF, HALF)) <= row((HALF, HALF))
    outs = []
    for h in range(4):
        at = slice(h * LANES, (h + 1) * LANES)
        q, one = query_of(queries, h)
        q = jnp.where(one, 1.0, q).astype(BF16)
        total = dot(weigh(dot_nt(q, ka_ref[:, at]), causal), va_ref[:, at])
        for b in range(2):
            keys = slice(b * 512, (b + 1) * 512)
            total += dot(weigh(dot_nt(q, ck_ref[keys, at])), cv_ref[keys, at])
        outs.append(divide(total, mask).astype(BF16))
    emit(jnp.concatenate(outs, axis=1), o_ref, (first, r1, r2, r3), 0)


def chunk_b(
    b0, b1, b2, b3, s1, s2, a0, a1, a2, a3, w_ref, o_ref, ck_ref, cv_ref, m_ref, ka_ref, va_ref, first, att_ref, late_ref, normed, kb, vb
):
    norm((b0, b1, b2, b3), (a0, a1, a2, a3), {1: s1, 2: s2}, normed, HALF + 16)
    kv, queries = project(normed, w_ref)
    late_ref[:, 0:512] = kv[HALF:]
    late_ref[:, 512:640] = queries[HALF:]
    kv, queries = kv[:HALF], queries[:HALF]
    mask = m_ref[HALF : 2 * HALF, :]
    kb[...] = as_keys(kv)
    vb[...] = as_values(kv, jnp.concatenate([mask] * 4, axis=1) > 0.0)
    causal = lane((HALF, HALF)) <= row((HALF, HALF))
    outs = []
    for h in range(4):
        at = slice(h * LANES, (h + 1) * LANES)
        q, one = query_of(queries, h)
        q = jnp.where(one, 1.0, q).astype(BF16)
        total = dot(weigh(dot_nt(q, kb[:, at]), causal), vb[:, at])
        total += dot(weigh(dot_nt(q, ka_ref[:, at])), va_ref[:, at])
        for b in range(2):
            keys = slice(b * 512, (b + 1) * 512)
            total += dot(weigh(dot_nt(q, ck_ref[keys, at])), cv_ref[keys, at])
        outs.append(divide(total, mask).astype(BF16))
    att = jnp.concatenate(outs, axis=1)
    att_ref[...] = att
    emit(att, o_ref, (first,), 0)


def decode(late_ref, o_ref, m_ref, len_ref, cache, first, r1, r2, r3, slab, total_ref, below_ref, sems):
    steps = [(d, b) for d in range(DEC) for b in range(2)]

    def copy(d, b):
        at = pl.ds(b * 512, 512)
        return pltpu.make_async_copy(cache.at[d + 1, at], slab.at[d, at], sems.at[d, b])

    for d, b in steps:

        @pl.when(b * 512 < len_ref[d + 1])
        def _():
            copy(d, b).start()

    fresh = late_ref[:, 0:512]
    late = jnp.concatenate([query_of(late_ref[:, 512:640], h)[0] for h in range(4)], axis=1)
    own = row((16, 512)) == lane((16, 512)) // LANES
    queries = []
    for d in range(DEC):
        q = jnp.where(own, jnp.broadcast_to(late[d : d + 1], (16, 512)), 0.0)
        queries.append(q.astype(BF16))
        new = jnp.broadcast_to(fresh[d : d + 1], (16, 512))
        live = m_ref[2 * HALF + d : 2 * HALF + d + 1, 0:1]
        self_score = jnp.sum(q * new, axis=1, keepdims=True) + 1.0
        self_weight = (self_score * self_score + 1.0) * live
        total_ref[d] = self_weight.astype(BF16).astype(F32) * new
        below_ref[d] = jnp.broadcast_to(self_weight + 2.0 * (1.0 - live), (16, 128))
    for d, b in steps:

        @pl.when(b * 512 < len_ref[d + 1])
        def _():
            copy(d, b).wait()
            keys = slab[d, b * 512 : (b + 1) * 512, :]
            score = dot_nt(queries[d], keys) + 1.0
            position = b * 512 + lane((16, 512))
            weight = jnp.where(position < len_ref[d + 1], score * score + 1.0, 0.0)
            total_ref[d] += dot(weight.astype(BF16), keys)
            below_ref[d] += jnp.broadcast_to(jnp.sum(weight, axis=1, keepdims=True), (16, 128))

    decoded = jnp.zeros((16, 512), F32)
    for d in range(DEC):
        live = m_ref[2 * HALF + d : 2 * HALF + d + 1, 0:1]
        ratio = live * total_ref[d] / below_ref[d][:, 0:1]
        value = jnp.sum(jnp.where(own, ratio, 0.0), axis=0, keepdims=True)
        decoded = jnp.where(row((16, 512)) == d, jnp.broadcast_to(value, (16, 512)), decoded)
    place = gray(lax.axis_index("col"))
    for s, out in enumerate((first, r1, r2, r3)):
        part = dot(decoded.astype(BF16), o_ref[gray((place + 3 - s) & 3)])
        out[...] = jnp.concatenate(
            [part[0:DEC, t * 128 : (t + 1) * 128] for t in range(4)], axis=0
        ).astype(out.dtype)


def unpack_sum(recv, part, out, base):
    for t in range(3):
        at = slice(t * HALF, (t + 1) * HALF)
        out[base : base + HALF, t * 128 : (t + 1) * 128] = (recv[at, :].astype(F32) + part[at, :]).astype(BF16)
    tail = recv[TAIL:BODY, :].astype(F32) + part[TAIL:BODY, :]
    out[base : base + HALF // 2, 384:448] = tail[:, 0:64].astype(BF16)
    out[base + HALF // 2 : base + HALF, 384:448] = tail[:, 64:128].astype(BF16)


def finish_a(recv, part, out):
    unpack_sum(recv, part, out, 0)


def finish(done, recv, part, back, own_late, out):
    out[:HALF, :] = done[...]
    unpack_sum(recv, part, out, HALF)
    late = recv[BODY:, :].astype(F32) + (back[...].astype(F32) + own_late[...])
    for t in range(4):
        width = 128 if t < 3 else 64
        rows = late[DEC * t : DEC * (t + 1), 0:width]
        out[SPAN_TOKENS:, t * 128 : t * 128 + width] = rows.astype(BF16)


def in_hbm(x):
    return pltpu.with_memory_space_constraint(x, pltpu.MemorySpace.HBM)


def after(value, *others):
    return lax.optimization_barrier((value, *others))[0]


def shards(hidden, norm_gain, qkv_weight, out_weight, cache, cached, token_mask):
    ring = [(gray(p), gray((p + 1) % 4)) for p in range(4)]

    def onward(x):
        return lax.ppermute(x, "col", ring)

    def across(x, k):
        return lax.ppermute(x, "row", [(i, i ^ k) for i in range(8)])

    a, b, own = call(
        pack,
        (shaped((BODY + 8, 128)), shaped((BODY + EXTRA, 128)), shaped((WROWS, 128))),
        [HBM] * 4,
        scratch=[pltpu.VMEM(x.shape, BF16) for x in (hidden, norm_gain, qkv_weight, out_weight)]
        + [pltpu.SemaphoreType.DMA((4,))],
        nbytes=300_000,
        name="pack",
    )(*(in_hbm(x) for x in (hidden, norm_gain, qkv_weight, out_weight)))
    plane = [own] + [across(own, k) for k in (2, 4, 6)]

    def sums(x, name):
        return call(square_b, shaped((HALF + 16, 128), F32), [VMEM], flops=COST_SQ, nbytes=300_000, name=name)(x)

    a1, b1 = onward(a), onward(b)
    a2, b2 = onward(a1), onward(b1)
    s1, s2 = sums(b1, "square_b1"), sums(b2, "square_b2")
    a3 = after(onward(after(a2, s1)), s2, *plane[1:])
    a, b = [a, a1, a2, a3], [b, b1, b2, onward(b2)]
    blocks = [own, across(after(own, s2), 1)]
    for block in plane[1:]:
        blocks += [block, across(block, 1)]
    w, o = call(
        place_weights,
        (shaped((4, 512, 640)), shaped((4, 512, 512))),
        [VMEM] * 8,
        nbytes=300_000,
        name="place_weights",
    )(*blocks)
    na = call(norm_a, shaped((HALF, 2048)), [VMEM] * 4, flops=COST_X, nbytes=300_000, name="norm_a")(*a)
    ck, cv = call(
        prepare_cache,
        (shaped((1024, 512)), shaped((1024, 512))),
        [HBM, SMEM],
        scratch=[pltpu.VMEM((1024, 512), BF16), pltpu.SemaphoreType.DMA],
        nbytes=300_000,
        name="prepare_cache",
        mib=12,
    )(in_hbm(cache), cached)
    mask = jnp.broadcast_to(token_mask.astype(F32)[:, None], (token_mask.shape[0], 128))
    parts = (shaped((BODY, 128), F32),) * 3
    wide, wire = shaped((HALF, 512)), shaped((BODY, 128))
    first, *rest_a, ka, va = call(
        chunk_a,
        (wire, *parts, wide, wide),
        [VMEM] * 6,
        flops=COST_CA,
        nbytes=300_000,
        name="chunk_a",
        mib=20,
    )(na, w, o, ck, cv, mask)
    send_a = onward(first)
    first, att, late = call(
        chunk_b,
        (wire, wide, shaped((16, 640), F32)),
        [VMEM] * 17,
        scratch=[
            pltpu.VMEM((HALF + 16, 2048), BF16),
            pltpu.VMEM((HALF, 512), BF16),
            pltpu.VMEM((HALF, 512), BF16),
        ],
        flops=COST_CB,
        nbytes=300_000,
        name="chunk_b",
        mib=20,
    )(*b, s1, s2, *a, w, o, ck, cv, mask, ka, va)
    send_b = onward(first)
    own_b = call(hop_3, parts[0], [VMEM] * 2, flops=COST_E, nbytes=300_000, name="hop_3")(att, o)

    few = shaped((EXTRA, 128), F32)
    back, *late = call(
        decode,
        (shaped((EXTRA, 128)), few, few, few),
        [VMEM] * 3 + [SMEM, HBM],
        scratch=[
            pltpu.VMEM((DEC, 1024, 512), BF16),
            pltpu.VMEM((DEC, 16, 512), F32),
            pltpu.VMEM((DEC, 16, 128), F32),
            pltpu.SemaphoreType.DMA((DEC, 2)),
        ],
        flops=COST_D,
        nbytes=300_000,
        name="decode",
        mib=12,
    )(late, o, mask, cached, in_hbm(cache))

    back = lax.ppermute(back, "col", [(gray((p + 1) % 4), gray(p)) for p in range(4)])

    def hop(body, recv, new, name):
        return onward(
            call(body, shaped((BODY + EXTRA, 128)), [VMEM] * 4, nbytes=300_000, name=name)(att, o, recv, new)
        )

    send_a = onward((send_a.astype(F32) + rest_a[0]).astype(BF16))
    send_b = hop(hop_1, send_b, late[0], "hop_1")
    send_a = onward((send_a.astype(F32) + rest_a[1]).astype(BF16))
    send_b = hop(hop_2, send_b, late[1], "hop_2")
    done = call(
        finish_a, shaped((HALF, hidden.shape[1])), [VMEM] * 2, flops=COST_F, nbytes=300_000, name="finish_a"
    )(send_a, rest_a[2])
    return call(finish, shaped(hidden.shape), [VMEM] * 5, flops=COST_G, nbytes=300_000, name="finish")(
        done, send_b, own_b, back, late[2]
    )


def taylor(taylor_score):
    return 1.0 + taylor_score + 0.5 * taylor_score * taylor_score


def attend(projected, cache, cached, token_mask):
    rows = projected.shape[0]
    width = 2 * FEATURE_WIDTH + HDIM
    lanes = FEATURE_WIDTH + HDIM
    heads_here = projected.shape[1] // width
    parts = projected.reshape(rows, heads_here, width)
    query_rows = parts[:, :, :FEATURE_WIDTH]
    key_rows = parts[:, :, FEATURE_WIDTH : 2 * FEATURE_WIDTH]
    values = parts[:, :, 2 * FEATURE_WIDTH :]
    store = cache.reshape(cache.shape[0], cache.shape[1], heads_here, lanes)
    capacity = cache.shape[1]
    block = min(512, capacity)
    score_scale = FEATURE_WIDTH ** (-0.5)
    live = token_mask.astype(jnp.float32)
    prefill_query_rows = query_rows[:SPAN_TOKENS]
    prior_tokens = store[0]
    offset = cached[0]

    def span_step(index, carry):
        numer, denom = carry
        span_slice = lax.dynamic_slice_in_dim(prior_tokens, index * block, block, 0)
        position = index * block + lax.iota(jnp.int32, block)
        taylor_score = (
            jnp.einsum(
                "sue,pue->usp",
                prefill_query_rows,
                span_slice[:, :, :FEATURE_WIDTH],
                preferred_element_type=jnp.float32,
            )
            * score_scale
        )
        weight = taylor(taylor_score) * (position < offset).astype(jnp.float32)[None, None, :]
        numer = numer + jnp.einsum(
            "hqk,khd->hqd",
            weight.astype(jnp.bfloat16),
            span_slice[:, :, FEATURE_WIDTH:],
            preferred_element_type=jnp.float32,
        )
        return (numer, denom + jnp.sum(weight, axis=-1))

    start_numer = jnp.zeros((heads_here, SPAN_TOKENS, HDIM), jnp.float32)
    start_denom = jnp.zeros((heads_here, SPAN_TOKENS), jnp.float32)
    span_blocks = (offset + block - 1) // block
    numer, denom = lax.fori_loop(0, span_blocks, span_step, (start_numer, start_denom))
    taylor_score = (
        jnp.einsum(
            "sue,pue->usp",
            prefill_query_rows,
            key_rows[:SPAN_TOKENS],
            preferred_element_type=jnp.float32,
        )
        * score_scale
    )
    order = lax.iota(jnp.int32, SPAN_TOKENS)
    allowed = (order[None, :] <= order[:, None]).astype(jnp.float32) * live[:SPAN_TOKENS][None, :]
    weight = taylor(taylor_score) * allowed[None]
    numer = numer + jnp.einsum(
        "hqk,khd->hqd",
        weight.astype(jnp.bfloat16),
        values[:SPAN_TOKENS],
        preferred_element_type=jnp.float32,
    )
    denom = denom + jnp.sum(weight, axis=-1)
    decode_queries = query_rows[SPAN_TOKENS:]
    past = store[1:]
    counts = cached[1:]

    def decode_step(index, carry):
        dec_numer, dec_denom = carry
        span_slice = lax.dynamic_slice_in_dim(past, index * block, block, 1)
        position = index * block + lax.iota(jnp.int32, block)
        taylor_score = (
            jnp.einsum(
                "rhf,rkhf->rhk",
                decode_queries,
                span_slice[..., :FEATURE_WIDTH],
                preferred_element_type=jnp.float32,
            )
            * score_scale
        )
        seen = (position[None, :] < counts[:, None]).astype(jnp.float32)
        weight = taylor(taylor_score) * seen[:, None, :]
        dec_numer = dec_numer + jnp.einsum(
            "rhk,rkhd->rhd",
            weight.astype(jnp.bfloat16),
            span_slice[..., FEATURE_WIDTH:],
            preferred_element_type=jnp.float32,
        )
        return (dec_numer, dec_denom + jnp.sum(weight, axis=-1))

    first_numer = jnp.zeros((DEC, heads_here, HDIM), jnp.float32)
    first_denom = jnp.zeros((DEC, heads_here), jnp.float32)
    decode_blocks = (jnp.max(counts) + block - 1) // block
    dec_numer, dec_denom = lax.fori_loop(0, decode_blocks, decode_step, (first_numer, first_denom))
    taylor_score = (
        jnp.sum(
            decode_queries.astype(jnp.float32) * key_rows[SPAN_TOKENS:].astype(jnp.float32), axis=-1
        )
        * score_scale
    )
    weight = taylor(taylor_score) * live[SPAN_TOKENS:, None]
    dec_numer = dec_numer + weight.astype(jnp.bfloat16).astype(jnp.float32)[..., None] * values[
        SPAN_TOKENS:
    ].astype(jnp.float32)
    dec_denom = dec_denom + weight
    numer_all = jnp.concatenate([jnp.transpose(numer, (1, 0, 2)), dec_numer], axis=0)
    denom_all = jnp.concatenate([jnp.transpose(denom, (1, 0)), dec_denom], axis=0)
    result = live[:, None, None] * numer_all / (denom_all + 1.0 - live[:, None])[..., None]
    return result.astype(jnp.bfloat16).reshape(rows, heads_here * HDIM)


def plain_shards(hidden, norm_gain, qkv_weight, out_weight, cache, cached, token_mask):
    full, gain = (
        lax.all_gather(hidden, "col", axis=1, tiled=True),
        lax.all_gather(norm_gain, "col", axis=0, tiled=True),
    )
    wide = full.astype(jnp.float32)
    normed = (
        wide
        * lax.rsqrt(jnp.mean(wide * wide, axis=-1, keepdims=True) + 1e-06)
        * gain.astype(jnp.float32)
    )
    normed = normed.astype(jnp.bfloat16)
    projected = jnp.dot(
        normed,
        lax.all_gather(qkv_weight, "row", axis=0, tiled=True),
        preferred_element_type=jnp.float32,
    ).astype(jnp.bfloat16)
    attended = attend(projected, cache, cached, token_mask)
    terms = jnp.dot(
        attended,
        lax.all_gather(out_weight, "row", axis=1, tiled=True),
        preferred_element_type=jnp.float32,
    )
    mixed = lax.psum_scatter(terms, "col", scatter_dimension=1, tiled=True).astype(jnp.bfloat16)
    return mixed


def solution(mesh):
    in_specs = (
        P("row", "col"),
        P("col"),
        P("row", "col"),
        P("col", "row"),
        P("row", None, "col"),
        P("row"),
        P("row"),
    )
    out_specs = P("row", "col")
    body = shards if (mesh.shape["row"], mesh.shape["col"]) == (8, 4) else plain_shards
    return jax.shard_map(body, mesh=mesh, in_specs=in_specs, out_specs=out_specs, check_vma=False)
```
